32 devices in a mesh: groups: 2 (over x), band: 16 (over z, y, core).
Axes of the slice: x: 2, y: 2, z: 4, core: 2. Of those that a mesh axis runs over, the one named last changes fastest.
Arguments:
- images: float32 [32, 8, 16, 32, 128], P(('groups', 'band')), parts along dimension 0, may hold values from -6 to 6
- coeffs: float32 [32, 8, 27, 3], P(('groups', 'band')), parts along dimension 0, may hold values from -3 to 3
- weights: float32 [32, 8], P(('groups', 'band')), parts along dimension 0, may hold values from 0.25 to 4
- scales: float32 [32, 8], P(('groups', 'band')), parts along dimension 0, may hold values from 0.5 to 2
- valid_epoch: int32 [32, 8], P(('groups', 'band')), parts along dimension 0, may hold values 0 or 1
- patch_owner: int32 [32, 8, 16, 1], P(('groups', 'band')), parts along dimension 0, may hold values from 0 to 15; in each aligned block of 128 rows (0 to 127, 128 to 255, ..., all dimensions but the last counted through in order) at most 16 rows name the same one
- patch_local: int32 [32, 8, 16], P(('groups', 'band')), parts along dimension 0, may hold values from 0 to 3
Outputs:
- difference: float32 [32, 8, 16, 32, 128], P(('groups', 'band')), parts along dimension 0
- templates: bfloat16 [128, 32, 128], P(('groups', 'band')), parts along dimension 0
The draws below stay inside these ranges and needn't reach their ends.
There are 2 independent parts, one for each index of `groups`. The reference program is written for one: setup_inputs(seed, part) draws one part's arguments, and reference() takes and returns one part's arrays. A program takes and returns all parts, laid end to end along the dimension named above; each array names one. Nothing has to cross between parts.
Inputs may be any that keep to these rules, and one draw needn't show every extreme that they name: `patch_owner`: no band sends more than 16 of its tiles to one owner, and some band sends exactly 16 tiles to some owner; every owner receives some tile.
All inputs are finite; a program needn't handle non-finite values. No bound on the sum of `valid_epoch` on one device may be relied on, other than what follows from the above.
Results may differ from the reference program's by a relative error of at most 0.0078.
Values may be sent and summed in bfloat16 or wider, within the bound.
No kernel may reach another device: no remote copies, remote signals or barrier semaphores. Data moves between devices by JAX's collectives and lax.ppermute only.
A program may use at most 64 MiB of HBM per device.

```python
import math
import jax
import jax.numpy as jnp
import numpy as np
from jax import lax

EPOCHS = 8
TD = 16
ROWS = 32
TILE = 128
PD = 4
HALF = 9
NB = 27
P_SIZE = 3
BANDS = 16
CAP = 16
PATCHES = 64
N_BAND = 16


def with_ends(entries, key, low, largest):
    longest = entries.shape.index(max(entries.shape))
    spots = []
    for shift in (0, 1):
        where = [jax.random.randint(jax.random.fold_in(key, axis), (), 0, length) for axis, length in enumerate(entries.shape)]
        where[longest] = (where[longest] + shift) % entries.shape[longest]
        spots.append(tuple(where))
    return entries.at[spots[0]].set(low).at[spots[1]].set(largest)


def levels(key, extent, split, least, largest):
    factor_of = 1.0
    for dim, shards_of in split:
        draws = jax.random.uniform(jax.random.fold_in(jax.random.fold_in(key, 6), dim), (shards_of,), jnp.float32, least / len(split), largest / len(split))
        factor_of = factor_of * jnp.repeat(jnp.exp(draws), extent[dim] // shards_of).reshape((-1,) + (1,) * (len(extent) - 1 - dim))
    return factor_of


def shared_out(rng, own, number, rows, number_of, top, reach, slope):
    sequence = jax.random.permutation(rng, number_of)
    packed, ordinary = load_shares(number_of, rows * top, reach, slope, True), load_shares(number_of, rows * top, reach, slope, False)
    places = jnp.arange(number_of)

    def named(tallies, turn):
        used = int((tallies > 0).sum())
        fixed = max(1, used // 4)
        shifted = fixed + (places - fixed + turn * (used - fixed)) % max(1, number_of - fixed)
        return jnp.zeros((number_of,), jnp.int32).at[sequence[jnp.where(places < fixed, places, shifted)]].set(jnp.asarray(tallies, jnp.int32))

    tallies = jnp.where(number % 4 == 0, named(packed, number // 4), named(ordinary, number - number // 4 - 1))
    mixed = jax.random.permutation(jax.random.fold_in(own, 3), number_of)
    donor, sink = mixed[0:number_of // 2 * 2:2], mixed[1:number_of // 2 * 2:2]
    margin = jnp.minimum(tallies[donor] - 1, reach - tallies[sink]) // 2
    margin = jnp.where((donor == sequence[0]) | (sink == sequence[0]) | (tallies[sink] == 0), 0, jnp.maximum(margin, 0))
    shifted = jax.random.randint(jax.random.fold_in(own, 4), (number_of // 2,), 0, 1 << 20) % (margin + 1)
    tallies = tallies.at[donor].add(-shifted).at[sink].add(shifted)
    members = jnp.searchsorted(jnp.cumsum(tallies), jnp.arange(rows * top), side="right").astype(jnp.int32)
    listing = members.reshape(top, rows).T
    listing = listing[jax.random.permutation(jax.random.fold_in(own, 1), rows)]
    turn = jax.random.randint(jax.random.fold_in(own, 2), (rows, 1), 0, top)
    return jnp.take_along_axis(listing, (jnp.arange(top)[None, :] + turn) % top, axis=1)


def load_shares(number_of, total, reach, skew, full):
    portions = [(1 << 20) // math.isqrt(standing ** skew) + 1 for standing in range(1, number_of + 1)]
    largest = reach if full else min(reach, max(-(-total // number_of), total * portions[0] // sum(portions)))
    least = 1 if total - largest >= number_of - 1 else 0
    holding, rest = [largest] + [least] * (number_of - 1), total - largest - least * (number_of - 1)
    while rest > 0:
        movable = [i for i in range(1, number_of) if holding[i] < largest] or [i for i in range(1, number_of) if holding[i] < reach]
        mass, budget = sum([portions[i] for i in movable]), rest
        for i in movable:
            addition = min(reach - holding[i], max(1, budget * portions[i] // mass), rest)
            holding[i] = holding[i] + addition
            rest = rest - addition
    return np.array(holding)


def bell_draw(key, dims, spread, most, split=(), held_as=jnp.bfloat16):
    values = spread * jax.random.normal(key, dims, jnp.float32)
    if split:
        values = values * levels(key, dims, split, -0.22, 0.18)
    return jnp.clip(values, -most, most).astype(held_as)


def setup_inputs(seed: int = 0, part: int = 0) -> dict:
    seeds = jax.random.split(jax.random.key(seed), 8)
    part_keys = jax.random.split(jax.random.fold_in(seeds[7], part), 8)
    images = bell_draw(part_keys[0], (BANDS, EPOCHS, TD, ROWS, TILE), 1.0, 6.0, ((0, 16),), jnp.float32)
    coeffs = bell_draw(part_keys[1], (BANDS, EPOCHS, NB, P_SIZE), 0.5, 3.0, ((0, 16),), jnp.float32)
    weights = jnp.clip(jnp.exp(math.log(4.0) - 2.7725887 * jax.random.uniform(part_keys[2], (BANDS, EPOCHS), jnp.float32) ** levels(part_keys[2], (BANDS, EPOCHS), ((0, 16),), -0.2, 0.2)), 0.25, 4.0)
    scales = jnp.clip(jnp.exp(math.log(2.0) - 1.3862944 * jax.random.uniform(part_keys[3], (BANDS, EPOCHS), jnp.float32) ** levels(part_keys[3], (BANDS, EPOCHS), ((0, 16),), -0.2, 0.2)), 0.5, 2.0)
    valid_epoch = with_ends((jax.random.randint(part_keys[4], (BANDS, EPOCHS), 0, 4) < 3).astype(jnp.int32), jax.random.fold_in(part_keys[4], 1), 0, 1)
    patch_owner_keys = jax.random.split(jax.random.fold_in(part_keys[5], 1), BANDS * EPOCHS * TD // (EPOCHS * TD))
    patch_owner_turns = jax.random.permutation(jax.random.fold_in(part_keys[5], 3), BANDS * EPOCHS * TD // (EPOCHS * TD))
    patch_owner = jax.vmap(lambda own, number: shared_out(jax.random.fold_in(part_keys[5], 2), own, number, EPOCHS * TD, N_BAND, 1, CAP, 2))(patch_owner_keys, patch_owner_turns).reshape((BANDS, EPOCHS, TD, 1))
    patch_local = with_ends(jax.random.randint(part_keys[6], (BANDS, EPOCHS, TD), 0, PD), jax.random.fold_in(part_keys[6], 1), 0, PD - 1).astype(jnp.int32)
    return dict(images=images, coeffs=coeffs, weights=weights, scales=scales, valid_epoch=valid_epoch, patch_owner=patch_owner, patch_local=patch_local)


sigmas = (0.75, 1.5, 3.0)
degrees = (4, 2, 2)


def kernel_matrices(tile_side):
    rows_out = lax.broadcasted_iota(jnp.int32, (tile_side, tile_side), 0)
    rows_in = lax.broadcasted_iota(jnp.int32, (tile_side, tile_side), 1)
    offset = (rows_out - rows_in).astype(jnp.float32)
    inside = (jnp.abs(rows_out - rows_in) <= HALF).astype(jnp.float32)
    taps = jnp.arange(-HALF, HALF + 1).astype(jnp.float32)
    tables = []
    for width_sigma, degree in zip(sigmas, degrees):
        normal_total = jnp.sum(jnp.exp(-taps * taps / (2.0 * width_sigma * width_sigma)))
        envelope = jnp.exp(-offset * offset / (2.0 * width_sigma * width_sigma)) * inside / normal_total
        for power in range(degree + 1):
            tables.append(envelope * (offset / width_sigma) ** power)
    return jnp.stack(tables)


def basis_pairs():
    kernel_list = []
    base_index = 0
    for degree in degrees:
        for column_power in range(degree + 1):
            for row_power in range(degree + 1 - column_power):
                kernel_list.append((base_index + row_power, base_index + column_power))
        base_index = base_index + degree + 1
    return kernel_list


def row_selector():
    kernel_list = basis_pairs()
    row_count = sum(degree + 1 for degree in degrees)
    table = np.zeros((len(kernel_list), row_count), np.float32)
    for basis_index, kernel_pair in enumerate(kernel_list):
        table[basis_index, kernel_pair[0]] = 1.0
    return jnp.asarray(table, jnp.float32)


def coordinates(per_epoch, tile_rows, tile_side):
    tile_index = lax.broadcasted_iota(jnp.float32, (per_epoch, tile_side), 0)
    column = lax.broadcasted_iota(jnp.float32, (per_epoch, tile_side), 1)
    across = 2.0 * (tile_index * tile_side + column + 0.5) / (per_epoch * tile_side) - 1.0
    down = 2.0 * (jnp.arange(tile_rows).astype(jnp.float32) + 0.5) / tile_rows - 1.0
    return across, down


def barrier_round(values):
    return lax.optimization_barrier(values.astype(jnp.bfloat16)).astype(jnp.float32)


def reference(images, coeffs, weights, scales, valid_epoch, patch_owner, patch_local):
    column_kernels = kernel_matrices(TILE)
    row_tables = barrier_round(kernel_matrices(ROWS))
    kernel_list = basis_pairs()
    column_stack = jnp.stack([column_kernels[kernel_pair[1]] for kernel_pair in kernel_list])
    selector = row_selector()
    row_count = column_kernels.shape[0]
    across, down = coordinates(TD, ROWS, TILE)

    def one_epoch(epoch_inputs):
        tile_stack, coef_epoch = epoch_inputs
        mixing = selector[:, :, None] * coef_epoch[:, None, :]
        combined = jnp.einsum('bjp,box->jxpo', mixing, column_stack, precision=lax.Precision.HIGHEST)
        mixer = barrier_round(combined.reshape(row_count * TILE, P_SIZE * TILE))
        pixels = barrier_round(tile_stack)
        rowed = barrier_round(jnp.einsum('jpy,tyx->tpjx', row_tables, pixels))
        flat = rowed.reshape(TD, ROWS, row_count * TILE)
        spatial = jnp.einsum('tpk,kq->tpq', flat, mixer).reshape(TD, ROWS, P_SIZE, TILE)
        return spatial[:, :, 0, :] + across[:, None, :] * spatial[:, :, 1, :] + down[None, :, None] * spatial[:, :, 2, :]

    def one_band(band_inputs):
        return lax.map(one_epoch, band_inputs)

    homogenized = lax.map(one_band, (images, coeffs))
    tile_count = EPOCHS * TD
    pixel_count = ROWS * TILE
    sent = barrier_round(homogenized).reshape(BANDS, tile_count, pixel_count)
    epoch_weight = barrier_round(weights * valid_epoch.astype(jnp.float32))
    tile_weight = jnp.broadcast_to(epoch_weight[:, :, None], (BANDS, EPOCHS, TD)).reshape(BANDS, tile_count)
    tile_scale = jnp.broadcast_to(scales[:, :, None], (BANDS, EPOCHS, TD)).reshape(BANDS, tile_count)
    global_patch = (patch_owner[..., 0] * PD + patch_local).reshape(BANDS, tile_count).astype(jnp.int32)

    def add_band(totals, band_inputs):
        band_sent, band_weight, band_patch = band_inputs
        return totals.at[band_patch].add(band_weight[:, None] * band_sent), None

    totals, unused = lax.scan(add_band, jnp.zeros((PATCHES, pixel_count), jnp.float32), (sent, tile_weight, global_patch))
    denominator = 1.0 + jax.ops.segment_sum(tile_weight.reshape(-1), global_patch.reshape(-1), num_segments=PATCHES)
    templates = (totals / denominator[:, None]).astype(jnp.bfloat16)
    template_values = lax.optimization_barrier(templates).astype(jnp.float32)
    matched = template_values[global_patch]
    difference = homogenized.reshape(BANDS, tile_count, pixel_count) - tile_scale[:, :, None] * matched
    return difference.reshape(BANDS, EPOCHS, TD, ROWS, TILE), templates.reshape(PATCHES, ROWS, TILE)
```

```python
import functools

import jax
import jax.numpy as jnp
import numpy as np
from jax import lax
from jax.experimental import pallas as pl
from jax.experimental.pallas import tpu as pltpu
from jax.sharding import PartitionSpec as P

PD = 4
HALF = 9
P_SIZE = 3

sigmas = (0.75, 1.5, 3.0)
degrees = (4, 2, 2)

BF16 = jnp.bfloat16
F32 = jnp.float32
EXTRA = 16


def kernel_matrices(tile_side):
    place = np.arange(tile_side)
    apart = place[:, None] - place[None, :]
    offset = apart.astype(np.float32)
    inside = (np.abs(apart) <= HALF).astype(np.float32)
    taps = np.arange(-HALF, HALF + 1).astype(np.float32)
    tables = []
    for width_sigma, degree in zip(sigmas, degrees):
        scale = np.float32(2.0 * width_sigma * width_sigma)
        total = np.sum(np.exp(-taps * taps / scale), dtype=np.float32)
        envelope = np.exp(-offset * offset / scale) * inside / total
        for power in range(degree + 1):
            tables.append((envelope * (offset / np.float32(width_sigma)) ** power).astype(np.float32))
    return np.stack(tables)


def basis_pairs():
    kernel_list = []
    base_index = 0
    for degree in degrees:
        for column_power in range(degree + 1):
            for row_power in range(degree + 1 - column_power):
                kernel_list.append((base_index + row_power, base_index + column_power))
        base_index = base_index + degree + 1
    return kernel_list


def stage_factors(band_count):
    factors = []
    rest = band_count
    if rest >= 2:
        factors.append(2)
        rest //= 2
    inner = 1
    while 4 * inner * inner <= rest:
        inner *= 2
    for factor in (inner, rest // inner):
        if factor > 1:
            factors.append(factor)
    return factors


def place_of(distance, factors):
    total = int(np.prod(factors))
    place = 0
    for factor in factors:
        total //= factor
        place = place + (distance % factor) * total
        distance = distance // factor
    return place


def smooth_kernel(
    me_ref, coef_ref, weight_ref, valid_ref, owner_ref, local_ref,
    image_ref, column_ref, row_ref, patch_row_ref, weight_row_ref,
    smooth_ref, *rest, factors, band_count, row_count,
):
    message_refs = rest[: factors[0]]
    mixer_ref, flat_ref, total_ref = rest[factors[0]:]
    epoch = pl.program_id(0)
    per_epoch, tile_rows, tile_side = image_ref.shape[1:]
    pairs = basis_pairs()

    @pl.when(epoch == 0)
    def _():
        total_ref[...] = jnp.zeros_like(total_ref)

    band_rows = 16
    for top in range(0, tile_side, band_rows):
        columns = [column_ref[c, top:top + band_rows, :] for c in range(row_count)]
        for r in range(row_count):
            used = [(b, pair[1]) for b, pair in enumerate(pairs) if pair[0] == r]
            for m in range(P_SIZE):
                value = None
                for b, c in used:
                    term = coef_ref[epoch, b * P_SIZE + m] * columns[c]
                    value = term if value is None else value + term
                mixer_ref[r * tile_side + top:r * tile_side + top + band_rows,
                          m * tile_side:(m + 1) * tile_side] = value.astype(BF16)

    for t in range(0, per_epoch, 2):
        pixels = jnp.concatenate([image_ref[0, t].astype(BF16), image_ref[0, t + 1].astype(BF16)], axis=1)
        rowed = jnp.dot(row_ref[...], pixels, preferred_element_type=F32).astype(BF16)
        for s in range(2):
            for r in range(row_count):
                flat_ref[(t + s) * tile_rows:(t + s + 1) * tile_rows,
                         r * tile_side:(r + 1) * tile_side] = (
                    rowed[r * tile_rows:(r + 1) * tile_rows, s * tile_side:(s + 1) * tile_side])

    spatial = jnp.dot(flat_ref[...], mixer_ref[...], preferred_element_type=F32)
    column = lax.broadcasted_iota(jnp.int32, (tile_rows, tile_side), 1).astype(F32)
    row = lax.broadcasted_iota(jnp.int32, (tile_rows, tile_side), 0).astype(F32)
    down = 2.0 * (row + 0.5) / tile_rows - 1.0
    weight = jnp.full((tile_rows, tile_side), weight_ref[0, epoch] * valid_ref[0, epoch].astype(F32), F32)
    weight = weight.astype(BF16).astype(F32)
    for t in range(per_epoch):
        across = 2.0 * (column + (t * tile_side + 0.5)) / (per_epoch * tile_side) - 1.0
        part = spatial[t * tile_rows:(t + 1) * tile_rows]
        value = (part[:, :tile_side] + across * part[:, tile_side:2 * tile_side]
                 + down * part[:, 2 * tile_side:])
        smooth_ref[0, t] = value
        place = place_of(owner_ref[epoch, t] ^ me_ref[0], factors) * PD + local_ref[epoch, t]
        total_ref[place] = total_ref[place] + weight * value.astype(BF16).astype(F32)

    @pl.when(epoch == pl.num_programs(0) - 1)
    def _():
        per_group = band_count // factors[0]
        lane_patch = patch_row_ref[...]
        lane_weight = weight_row_ref[...]
        line = lax.broadcasted_iota(jnp.int32, (EXTRA, lane_patch.shape[1]), 0)
        for g in range(factors[0]):
            @pl.loop(0, per_group)
            def _(i):
                block = g * per_group + i
                for q in range(PD):
                    message_refs[g][i, q * tile_rows:(q + 1) * tile_rows, :] = total_ref[block * PD + q].astype(BF16)
                named = (line < PD) & (lane_patch == block * PD + line)
                marks = jnp.where(named, lane_weight, 0.0)
                folded = marks[:, :tile_side]
                for k in range(1, marks.shape[1] // tile_side):
                    folded = folded + marks[:, k * tile_side:(k + 1) * tile_side]
                message_refs[g][i, PD * tile_rows:, :] = folded.astype(BF16)


def smooth(me, coeffs, weights, valid_epoch, owners, locals_, images, patch_row, weight_row, factors, band_count):
    _, epochs, per_epoch, tile_rows, tile_side = images.shape
    columns = np.ascontiguousarray(kernel_matrices(tile_side).transpose(0, 2, 1))
    row_count = columns.shape[0]
    rows = jnp.asarray(kernel_matrices(tile_rows).reshape(row_count * tile_rows, tile_rows), BF16)
    block_rows = PD * tile_rows + EXTRA
    per_group = band_count // factors[0]
    smem = pl.BlockSpec(memory_space=pltpu.SMEM)
    tile_block = pl.BlockSpec((1, per_epoch, tile_rows, tile_side), lambda e: (e, 0, 0, 0))

    def whole(shape):
        return pl.BlockSpec(shape, lambda e: (0,) * len(shape), pipeline_mode=pl.Buffered(1))

    message = jax.ShapeDtypeStruct((per_group, block_rows, tile_side), BF16)
    return pl.pallas_call(
        functools.partial(smooth_kernel, factors=factors, band_count=band_count, row_count=row_count),
        grid=(epochs,),
        in_specs=[smem] * 6 + [
            tile_block, whole(columns.shape), whole(rows.shape), whole(patch_row.shape), whole(weight_row.shape),
        ],
        out_specs=[tile_block] + [pl.BlockSpec(message.shape, lambda e: (0, 0, 0))] * factors[0],
        out_shape=[jax.ShapeDtypeStruct(images.shape[1:], F32)] + [message] * factors[0],
        scratch_shapes=[
            pltpu.VMEM((row_count * tile_side, P_SIZE * tile_side), BF16),
            pltpu.VMEM((per_epoch * tile_rows, row_count * tile_side), BF16),
            pltpu.VMEM((band_count * PD, tile_rows, tile_side), F32),
        ],
        compiler_params=pltpu.CompilerParams(
            dimension_semantics=("arbitrary",), vmem_limit_bytes=40 * 1024 * 1024),
        name="smooth",
    )(me, coeffs, weights, valid_epoch, owners, locals_, images[0], jnp.asarray(columns), rows, patch_row, weight_row)


def add_kernel(*refs, count, groups):
    parts, outs = refs[:count], refs[count:]
    per_group = outs[0].shape[0]
    for g in range(groups):
        @pl.loop(0, per_group)
        def _(i):
            total = parts[0][g * per_group + i].astype(F32)
            for part in parts[1:]:
                total = total + part[g * per_group + i].astype(F32)
            outs[g][i] = total.astype(BF16)


def add_and_split(parts, groups):
    blocks, block_rows, lanes = parts[0].shape
    out = jax.ShapeDtypeStruct((blocks // groups, block_rows, lanes), BF16)
    return pl.pallas_call(
        functools.partial(add_kernel, count=len(parts), groups=groups),
        out_shape=[out] * groups, name="add_and_split",
    )(*parts)


def finish_kernel(*refs, tile_rows):
    parts, out_ref = refs[:-1], refs[-1]
    total = parts[0][0].astype(F32)
    for part in parts[1:]:
        total = total + part[0].astype(F32)
    for q in range(PD):
        mass = jnp.sum(total[PD * tile_rows + q:PD * tile_rows + q + 1, :], axis=1, keepdims=True)
        out_ref[q] = (total[q * tile_rows:(q + 1) * tile_rows] / (1.0 + mass)).astype(BF16)


def finish(parts, tile_rows):
    lanes = parts[0].shape[2]
    return pl.pallas_call(
        functools.partial(finish_kernel, tile_rows=tile_rows),
        out_shape=jax.ShapeDtypeStruct((PD, tile_rows, lanes), BF16), name="finish",
    )(*parts)


def difference_kernel(me_ref, scale_ref, owner_ref, local_ref, table_ref, smooth_ref, out_ref, *, factors):
    epoch = pl.program_id(0)
    scale = scale_ref[0, epoch]
    for t in range(smooth_ref.shape[1]):
        place = place_of(owner_ref[epoch, t] ^ me_ref[0], factors) * PD + local_ref[epoch, t]
        out_ref[0, t] = smooth_ref[0, t] - scale * table_ref[place].astype(F32)


def subtract(me, scales, owners, locals_, table, smoothed, factors):
    epochs, per_epoch, tile_rows, tile_side = smoothed.shape
    smem = pl.BlockSpec(memory_space=pltpu.SMEM)
    tile_block = pl.BlockSpec((1, per_epoch, tile_rows, tile_side), lambda e: (e, 0, 0, 0))
    return pl.pallas_call(
        functools.partial(difference_kernel, factors=factors),
        grid=(epochs,),
        in_specs=[smem] * 4 + [
            pl.BlockSpec(table.shape, lambda e: (0, 0, 0), pipeline_mode=pl.Buffered(1)), tile_block],
        out_specs=tile_block,
        out_shape=jax.ShapeDtypeStruct(smoothed.shape, F32),
        compiler_params=pltpu.CompilerParams(dimension_semantics=("arbitrary",)),
        name="subtract",
    )(me, scales, owners, locals_, table, smoothed)


def body(images, coeffs, weights, scales, valid_epoch, patch_owner, patch_local):
    band_count = lax.axis_size("band")
    _, epochs, per_epoch, tile_rows, tile_side = images.shape
    tile_count = epochs * per_epoch
    factors = stage_factors(band_count)
    me = lax.axis_index("band").astype(jnp.int32).reshape(1)
    owners = patch_owner.reshape(epochs, per_epoch)
    locals_ = patch_local.reshape(epochs, per_epoch)
    flat_coeffs = coeffs.reshape(epochs, -1)
    patch_row = (place_of(owners ^ me[0], factors) * PD + locals_).reshape(1, tile_count)
    weight_row = jnp.broadcast_to(
        (weights[0] * valid_epoch[0].astype(F32)).astype(BF16).astype(F32)[:, None], (epochs, per_epoch)
    ).reshape(1, tile_count)

    smoothed, *blocks = smooth(
        me, flat_coeffs, weights, valid_epoch, owners, locals_, images, patch_row, weight_row, factors, band_count)

    def exchange(value, step):
        return lax.ppermute(value, "band", [(d, d ^ step) for d in range(band_count)])

    stride = 1
    strides = []
    for k, factor in enumerate(factors):
        strides.append(stride)
        parts = [blocks[0]] + [exchange(blocks[j], j * stride) for j in range(1, factor)]
        stride *= factor
        if k + 1 < len(factors):
            blocks = add_and_split(parts, factors[k + 1])
    templates = finish(parts, tile_rows)

    table = templates
    for factor, stride in zip(reversed(factors), reversed(strides)):
        table = jnp.concatenate([table] + [exchange(table, j * stride) for j in range(1, factor)], axis=0)

    difference = subtract(me, scales, owners, locals_, table, smoothed, factors)
    return difference[None], templates


def solution(mesh):
    return jax.shard_map(
        body,
        mesh=mesh,
        in_specs=(
            P(("groups", "band"), None, None, None, None),
            P(("groups", "band"), None, None, None),
            P(("groups", "band"), None),
            P(("groups", "band"), None),
            P(("groups", "band"), None),
            P(("groups", "band"), None, None, None),
            P(("groups", "band"), None, None),
        ),
        out_specs=(
            P(("groups", "band"), None, None, None, None),
            P(("groups", "band"), None, None),
        ),
        check_vma=False,
    )
```

```python
import functools

import jax
import jax.numpy as jnp
import numpy as np
from jax import lax
from jax.experimental import pallas as pl
from jax.experimental.pallas import tpu as pltpu
from jax.sharding import PartitionSpec as P

PD = 4
HALF = 9
P_SIZE = 3

sigmas = (0.75, 1.5, 3.0)
degrees = (4, 2, 2)

BF16 = jnp.bfloat16
F32 = jnp.float32
EXTRA = 16


def kernel_matrices(tile_side):
    place = np.arange(tile_side)
    apart = place[:, None] - place[None, :]
    offset = apart.astype(np.float32)
    inside = (np.abs(apart) <= HALF).astype(np.float32)
    taps = np.arange(-HALF, HALF + 1).astype(np.float32)
    tables = []
    for width_sigma, degree in zip(sigmas, degrees):
        scale = np.float32(2.0 * width_sigma * width_sigma)
        total = np.sum(np.exp(-taps * taps / scale), dtype=np.float32)
        envelope = np.exp(-offset * offset / scale) * inside / total
        for power in range(degree + 1):
            tables.append((envelope * (offset / np.float32(width_sigma)) ** power).astype(np.float32))
    return np.stack(tables)


def basis_pairs():
    kernel_list = []
    base_index = 0
    for degree in degrees:
        for column_power in range(degree + 1):
            for row_power in range(degree + 1 - column_power):
                kernel_list.append((base_index + row_power, base_index + column_power))
        base_index = base_index + degree + 1
    return kernel_list


def stage_factors(band_count):
    factors = []
    rest = band_count
    if rest >= 2:
        factors.append(2)
        rest //= 2
    inner = 1
    while 4 * inner * inner <= rest:
        inner *= 2
    for factor in (inner, rest // inner):
        if factor > 1:
            factors.append(factor)
    return factors


def place_of(distance, factors):
    total = int(np.prod(factors))
    place = 0
    for factor in factors:
        total //= factor
        place = place + (distance & (factor - 1)) * total
        distance = distance >> (factor.bit_length() - 1)
    return place


def smooth_kernel(
    me_ref, coef_ref, weight_ref, valid_ref, owner_ref, local_ref, image_ref, column_ref, row_ref,
    smooth_ref, *rest, factors, band_count, row_count,
):
    message_refs = rest[: factors[0]]
    mixer_ref, flat_ref, total_ref = rest[factors[0]:]
    epoch = pl.program_id(0)
    per_epoch, tile_rows, tile_side = image_ref.shape[1:]
    pairs = basis_pairs()

    @pl.when(epoch == 0)
    def _():
        total_ref[...] = jnp.zeros_like(total_ref)

    band_rows = 16
    for top in range(0, tile_side, band_rows):
        columns = [column_ref[c, top:top + band_rows, :] for c in range(row_count)]
        for r in range(row_count):
            used = [(b, pair[1]) for b, pair in enumerate(pairs) if pair[0] == r]
            for m in range(P_SIZE):
                value = None
                for b, c in used:
                    term = coef_ref[m, epoch, b] * columns[c]
                    value = term if value is None else value + term
                mixer_ref[r * tile_side + top:r * tile_side + top + band_rows,
                          m * tile_side:(m + 1) * tile_side] = value.astype(BF16)

    for t in range(0, per_epoch, 2):
        pixels = jnp.concatenate([image_ref[0, t].astype(BF16), image_ref[0, t + 1].astype(BF16)], axis=1)
        rowed = jnp.dot(row_ref[...], pixels, preferred_element_type=F32).astype(BF16)
        for s in range(2):
            for r in range(row_count):
                flat_ref[(t + s) * tile_rows:(t + s + 1) * tile_rows,
                         r * tile_side:(r + 1) * tile_side] = (
                    rowed[r * tile_rows:(r + 1) * tile_rows, s * tile_side:(s + 1) * tile_side])

    spatial = jnp.dot(flat_ref[...], mixer_ref[...], preferred_element_type=F32)
    column = lax.broadcasted_iota(jnp.int32, (tile_rows, tile_side), 1).astype(F32)
    row = lax.broadcasted_iota(jnp.int32, (tile_rows, tile_side), 0).astype(F32)
    down = 2.0 * (row + 0.5) / tile_rows - 1.0
    lane = lax.broadcasted_iota(jnp.int32, (8, tile_side), 1)
    weight = jnp.full((8, tile_side), weight_ref[0, epoch] * valid_ref[0, epoch].astype(F32), F32)
    weight = weight.astype(BF16).astype(F32)
    weights = jnp.concatenate([weight] * (tile_rows // 8), axis=0)
    for t in range(per_epoch):
        across = 2.0 * (column + (t * tile_side + 0.5)) / (per_epoch * tile_side) - 1.0
        part = spatial[t * tile_rows:(t + 1) * tile_rows]
        value = (part[:, :tile_side] + across * part[:, tile_side:2 * tile_side]
                 + down * part[:, 2 * tile_side:])
        smooth_ref[epoch, t] = value
        place = place_of(owner_ref[epoch, t] ^ me_ref[0], factors) * PD + local_ref[epoch, t]
        total_ref[place, :tile_rows] = total_ref[place, :tile_rows] + weights * value.astype(BF16).astype(F32)
        total_ref[place, tile_rows:] = total_ref[place, tile_rows:] + jnp.where(lane == t % tile_side, weight, 0.0)

    @pl.when(epoch == pl.num_programs(0) - 1)
    def _():
        per_group = band_count // factors[0]
        line = lax.broadcasted_iota(jnp.int32, (8, tile_side), 0)
        for g in range(factors[0]):
            @pl.loop(0, per_group)
            def _(i):
                block = (g * per_group + i) * PD
                marks = jnp.zeros((8, tile_side), F32)
                for q in range(PD):
                    message_refs[g][i, q * tile_rows:(q + 1) * tile_rows, :] = (
                        total_ref[block + q, :tile_rows].astype(BF16))
                    marks = jnp.where(line == q, total_ref[block + q, tile_rows:], marks)
                message_refs[g][i, PD * tile_rows:, :] = (
                    jnp.concatenate([marks, jnp.zeros((EXTRA - 8, tile_side), F32)], axis=0).astype(BF16))


VMEM = pl.BlockSpec(memory_space=pltpu.VMEM)
SMEM = pl.BlockSpec(memory_space=pltpu.SMEM)


def smooth(me, coeffs, weights, valid_epoch, owners, locals_, images, factors, band_count):
    epochs, per_epoch, tile_rows, tile_side = images.shape
    columns = np.ascontiguousarray(kernel_matrices(tile_side).transpose(0, 2, 1))
    row_count = columns.shape[0]
    rows = jnp.asarray(kernel_matrices(tile_rows).reshape(row_count * tile_rows, tile_rows), BF16)
    block_rows = PD * tile_rows + EXTRA
    per_group = band_count // factors[0]
    tile_block = pl.BlockSpec((1, per_epoch, tile_rows, tile_side), lambda e: (e, 0, 0, 0))

    def whole(shape):
        return pl.BlockSpec(shape, lambda e: (0,) * len(shape), pipeline_mode=pl.Buffered(1))

    message = jax.ShapeDtypeStruct((per_group, block_rows, tile_side), BF16)
    return pl.pallas_call(
        functools.partial(smooth_kernel, factors=factors, band_count=band_count, row_count=row_count),
        grid=(epochs,),
        in_specs=[SMEM] * 6 + [tile_block, whole(columns.shape), whole(rows.shape)],
        out_specs=[VMEM] * (1 + factors[0]),
        out_shape=[jax.ShapeDtypeStruct(images.shape, F32)] + [message] * factors[0],
        scratch_shapes=[
            pltpu.VMEM((row_count * tile_side, P_SIZE * tile_side), BF16),
            pltpu.VMEM((per_epoch * tile_rows, row_count * tile_side), BF16),
            pltpu.VMEM((band_count * PD, tile_rows + 8, tile_side), F32),
        ],
        compiler_params=pltpu.CompilerParams(
            dimension_semantics=("arbitrary",), vmem_limit_bytes=VMEM_SMOOTH),
        name="smooth",
    )(me, *[pltpu.with_memory_space_constraint(value, pltpu.HBM) for value in (
        coeffs, weights, valid_epoch, owners, locals_, images, jnp.asarray(columns), rows)])


def add_kernel(*refs, count, groups):
    parts, outs = refs[:count], refs[count:]
    per_group = outs[0].shape[0]
    for g in range(groups):
        for i in range(per_group):
            total = parts[0][g * per_group + i].astype(F32)
            for part in parts[1:]:
                total = total + part[g * per_group + i].astype(F32)
            outs[g][i] = total.astype(BF16)


def add_and_split(parts, groups):
    blocks, block_rows, lanes = parts[0].shape
    out = jax.ShapeDtypeStruct((blocks // groups, block_rows, lanes), BF16)
    return pl.pallas_call(
        functools.partial(add_kernel, count=len(parts), groups=groups),
        in_specs=[VMEM] * len(parts), out_specs=[VMEM] * groups,
        out_shape=[out] * groups, name="add_and_split",
        compiler_params=pltpu.CompilerParams(vmem_limit_bytes=VMEM_SMALL),
    )(*parts)


def finish_kernel(*refs, tile_rows):
    parts, out_ref = refs[:-1], refs[-1]
    total = parts[0][0].astype(F32)
    for part in parts[1:]:
        total = total + part[0].astype(F32)
    for q in range(PD):
        mass = jnp.sum(total[PD * tile_rows + q:PD * tile_rows + q + 1, :], axis=1, keepdims=True)
        out_ref[q] = (total[q * tile_rows:(q + 1) * tile_rows] / (1.0 + mass)).astype(BF16)


def finish(parts, tile_rows):
    lanes = parts[0].shape[2]
    return pl.pallas_call(
        functools.partial(finish_kernel, tile_rows=tile_rows),
        in_specs=[VMEM] * len(parts), out_specs=VMEM,
        out_shape=jax.ShapeDtypeStruct((PD, tile_rows, lanes), BF16), name="finish",
        compiler_params=pltpu.CompilerParams(vmem_limit_bytes=VMEM_SMALL),
    )(*parts)


def difference_kernel(me_ref, scale_ref, owner_ref, local_ref, smooth_ref, *rest, factors, count):
    pieces, (out_ref, table_ref) = rest[:count], rest[count:]
    epoch = pl.program_id(0)

    @pl.when(epoch == 0)
    def _():
        start = 0
        for piece in pieces:
            table_ref[start:start + piece.shape[0]] = piece[...]
            start += piece.shape[0]

    scale = scale_ref[0, epoch]
    for t in range(smooth_ref.shape[1]):
        place = place_of(owner_ref[epoch, t] ^ me_ref[0], factors) * PD + local_ref[epoch, t]
        out_ref[0, t] = smooth_ref[epoch, t] - scale * table_ref[place].astype(F32)


def subtract(me, scales, owners, locals_, pieces, smoothed, factors):
    epochs, per_epoch, tile_rows, tile_side = smoothed.shape
    tile_block = pl.BlockSpec((1, per_epoch, tile_rows, tile_side), lambda e: (e, 0, 0, 0))
    patches = sum(piece.shape[0] for piece in pieces)
    return pl.pallas_call(
        functools.partial(difference_kernel, factors=factors, count=len(pieces)),
        grid=(epochs,),
        in_specs=[SMEM] * 4 + [VMEM] * (1 + len(pieces)),
        out_specs=tile_block,
        out_shape=jax.ShapeDtypeStruct(smoothed.shape, F32),
        scratch_shapes=[pltpu.VMEM((patches, tile_rows, tile_side), BF16)],
        compiler_params=pltpu.CompilerParams(
            dimension_semantics=("arbitrary",), vmem_limit_bytes=VMEM_SUBTRACT),
        name="subtract",
    )(me, scales, owners, locals_, smoothed, *pieces)


VMEM_SMOOTH = 48 * 1024 * 1024
VMEM_SMALL = 16 * 1024 * 1024
VMEM_SUBTRACT = 40 * 1024 * 1024


def body(images, coeffs, weights, scales, valid_epoch, patch_owner, patch_local):
    band_count = lax.axis_size("band")
    _, epochs, per_epoch, tile_rows, tile_side = images.shape
    factors = stage_factors(band_count)
    me = lax.axis_index("band").astype(jnp.int32).reshape(1)
    owners = patch_owner.reshape(epochs, per_epoch)
    locals_ = patch_local.reshape(epochs, per_epoch)

    smoothed, *blocks = smooth(
        me, coeffs[0].transpose(2, 0, 1), weights, valid_epoch, owners, locals_, images[0], factors, band_count)

    def exchange(value, step):
        return lax.ppermute(value, "band", [(d, d ^ step) for d in range(band_count)])

    stride = 1
    strides = []
    for k, factor in enumerate(factors):
        strides.append(stride)
        parts = [blocks[0]] + [exchange(blocks[j], j * stride) for j in range(1, factor)]
        stride *= factor
        if k + 1 < len(factors):
            blocks = add_and_split(parts, factors[k + 1])
    templates = finish(parts, tile_rows)

    pieces = [templates]
    for factor, stride in zip(reversed(factors), reversed(strides)):
        if stride > 1 and len(pieces) > 1:
            pieces = [jnp.concatenate(pieces, axis=0)]
        pieces = pieces + [exchange(piece, j * stride) for j in range(1, factor) for piece in pieces]

    difference = subtract(me, scales, owners, locals_, pieces, smoothed, factors)
    return difference[None], templates


def solution(mesh):
    return jax.shard_map(
        body,
        mesh=mesh,
        in_specs=(
            P(("groups", "band"), None, None, None, None),
            P(("groups", "band"), None, None, None),
            P(("groups", "band"), None),
            P(("groups", "band"), None),
            P(("groups", "band"), None),
            P(("groups", "band"), None, None, None),
            P(("groups", "band"), None, None),
        ),
        out_specs=(
            P(("groups", "band"), None, None, None, None),
            P(("groups", "band"), None, None),
        ),
        check_vma=False,
    )
```

```python
import functools

import jax
import jax.numpy as jnp
import numpy as np
from jax import lax
from jax.experimental import pallas as pl
from jax.experimental.pallas import tpu as pltpu
from jax.sharding import PartitionSpec as P

PD = 4
HALF = 9
P_SIZE = 3

sigmas = (0.75, 1.5, 3.0)
degrees = (4, 2, 2)

BF16 = jnp.bfloat16
F32 = jnp.float32
EXTRA = 16


def kernel_matrices(tile_side):
    place = np.arange(tile_side)
    apart = place[:, None] - place[None, :]
    offset = apart.astype(np.float32)
    inside = (np.abs(apart) <= HALF).astype(np.float32)
    taps = np.arange(-HALF, HALF + 1).astype(np.float32)
    tables = []
    for width_sigma, degree in zip(sigmas, degrees):
        scale = np.float32(2.0 * width_sigma * width_sigma)
        total = np.sum(np.exp(-taps * taps / scale), dtype=np.float32)
        envelope = np.exp(-offset * offset / scale) * inside / total
        for power in range(degree + 1):
            tables.append((envelope * (offset / np.float32(width_sigma)) ** power).astype(np.float32))
    return np.stack(tables)


def basis_pairs():
    kernel_list = []
    base_index = 0
    for degree in degrees:
        for column_power in range(degree + 1):
            for row_power in range(degree + 1 - column_power):
                kernel_list.append((base_index + row_power, base_index + column_power))
        base_index = base_index + degree + 1
    return kernel_list


def stage_factors(band_count):
    factors = []
    rest = band_count
    if rest >= 2:
        factors.append(2)
        rest //= 2
    inner = 1
    while 4 * inner * inner <= rest:
        inner *= 2
    for factor in (inner, rest // inner):
        if factor > 1:
            factors.append(factor)
    return factors


def place_of(distance, factors):
    total = int(np.prod(factors))
    place = 0
    for factor in factors:
        total //= factor
        place = place + (distance & (factor - 1)) * total
        distance = distance >> (factor.bit_length() - 1)
    return place


def smooth_kernel(
    me_ref, coef_ref, weight_ref, valid_ref, owner_ref, local_ref, image_ref, column_ref, row_ref,
    smooth_ref, *rest, factors, band_count, row_count,
):
    message_refs = rest[: factors[0]]
    mixer_ref, column_pass_ref, total_ref = rest[factors[0]:]
    epoch = pl.program_id(0)
    per_epoch, tile_rows, tile_side = image_ref.shape[1:]
    per_lanes = tile_side // tile_rows
    pairs = basis_pairs()

    @pl.when(epoch == 0)
    def _():
        total_ref[...] = jnp.zeros_like(total_ref)

    row = lax.broadcasted_iota(jnp.int32, (tile_rows, tile_side), 0).astype(F32)
    down = 2.0 * (row + 0.5) / tile_rows - 1.0
    for block in range(mixer_ref.shape[0]):
        used = [b for b, pair in enumerate(pairs) if pair[1] // per_lanes == block]
        sums = []
        for m in range(P_SIZE):
            value = None
            for b in used:
                term = coef_ref[m, epoch, b] * row_ref[b]
                value = term if value is None else value + term
            sums.append(value)
        mixer_ref[block, :tile_rows] = (sums[0] + down * sums[2]).astype(BF16)
        mixer_ref[block, tile_rows:] = sums[1].astype(BF16)

    pixels = image_ref[0].reshape(per_epoch * tile_rows, tile_side).astype(BF16)
    for c in range(0, row_count, 2):
        wide = min(2, row_count - c)
        passed = jnp.dot(
            pixels, column_ref[:, c * tile_side:(c + wide) * tile_side], preferred_element_type=F32).astype(BF16)
        for s in range(wide):
            for t in range(per_epoch):
                column_pass_ref[t, (c + s) * tile_rows:(c + s + 1) * tile_rows] = (
                    passed[t * tile_rows:(t + 1) * tile_rows, s * tile_side:(s + 1) * tile_side])

    depth = row_count * tile_rows
    mixer = jnp.concatenate([mixer_ref[block] for block in range(mixer_ref.shape[0])], axis=1)[:, :depth]
    column = lax.broadcasted_iota(jnp.int32, (tile_rows, tile_side), 1).astype(F32)
    lane = lax.broadcasted_iota(jnp.int32, (8, tile_side), 1)
    weight = jnp.full((8, tile_side), weight_ref[0, epoch] * valid_ref[0, epoch].astype(F32), F32)
    weight = weight.astype(BF16).astype(F32)
    weights = jnp.concatenate([weight] * (tile_rows // 8), axis=0)
    for first in range(0, per_epoch, 2):
        both = jnp.concatenate([column_pass_ref[first], column_pass_ref[first + 1]], axis=1)
        spatial = jnp.dot(mixer, both, preferred_element_type=F32)
        for s in range(2):
            t = first + s
            across = 2.0 * (column + (t * tile_side + 0.5)) / (per_epoch * tile_side) - 1.0
            part = spatial[:, s * tile_side:(s + 1) * tile_side]
            value = part[:tile_rows] + across * part[tile_rows:]
            smooth_ref[epoch, t] = value
            place = place_of(owner_ref[epoch, t] ^ me_ref[0], factors) * PD + local_ref[epoch, t]
            total_ref[place, :tile_rows] = total_ref[place, :tile_rows] + weights * value.astype(BF16).astype(F32)
            total_ref[place, tile_rows:] = (
                total_ref[place, tile_rows:] + jnp.where(lane == t % tile_side, weight, 0.0))

    @pl.when(epoch == pl.num_programs(0) - 1)
    def _():
        per_group = band_count // factors[0]
        line = lax.broadcasted_iota(jnp.int32, (8, tile_side), 0)
        for g in range(factors[0]):
            @pl.loop(0, per_group)
            def _(i):
                block = (g * per_group + i) * PD
                marks = jnp.zeros((8, tile_side), F32)
                for q in range(PD):
                    message_refs[g][i, q * tile_rows:(q + 1) * tile_rows, :] = (
                        total_ref[block + q, :tile_rows].astype(BF16))
                    marks = jnp.where(line == q, total_ref[block + q, tile_rows:], marks)
                message_refs[g][i, PD * tile_rows:, :] = (
                    jnp.concatenate([marks, jnp.zeros((EXTRA - 8, tile_side), F32)], axis=0).astype(BF16))


VMEM = pl.BlockSpec(memory_space=pltpu.VMEM)
SMEM = pl.BlockSpec(memory_space=pltpu.SMEM)


def smooth(me, coeffs, weights, valid_epoch, owners, locals_, images, factors, band_count):
    epochs, per_epoch, tile_rows, tile_side = images.shape
    columns = kernel_matrices(tile_side)
    row_count = columns.shape[0]
    columns = jnp.asarray(columns.transpose(2, 0, 1).reshape(tile_side, row_count * tile_side), BF16)
    per_lanes = tile_side // tile_rows
    row_matrices = np.asarray(kernel_matrices(tile_rows), dtype=BF16).astype(np.float32)
    pairs = basis_pairs()
    rows = np.zeros((len(pairs), tile_rows, tile_side), np.float32)
    for b, (row, column) in enumerate(pairs):
        start = column % per_lanes * tile_rows
        rows[b, :, start:start + tile_rows] = row_matrices[row]
    block_rows = PD * tile_rows + EXTRA
    per_group = band_count // factors[0]
    tile_block = pl.BlockSpec((1, per_epoch, tile_rows, tile_side), lambda e: (e, 0, 0, 0))

    def whole(shape):
        return pl.BlockSpec(shape, lambda e: (0,) * len(shape), pipeline_mode=pl.Buffered(1))

    message = jax.ShapeDtypeStruct((per_group, block_rows, tile_side), BF16)
    return pl.pallas_call(
        functools.partial(smooth_kernel, factors=factors, band_count=band_count, row_count=row_count),
        grid=(epochs,),
        in_specs=[SMEM] * 6 + [tile_block, whole(columns.shape), whole(rows.shape)],
        out_specs=[VMEM] * (1 + factors[0]),
        out_shape=[jax.ShapeDtypeStruct(images.shape, F32)] + [message] * factors[0],
        scratch_shapes=[
            pltpu.VMEM((-(-row_count // per_lanes), 2 * tile_rows, tile_side), BF16),
            pltpu.VMEM((per_epoch, row_count * tile_rows, tile_side), BF16),
            pltpu.VMEM((band_count * PD, tile_rows + 8, tile_side), F32),
        ],
        compiler_params=pltpu.CompilerParams(
            dimension_semantics=("arbitrary",), vmem_limit_bytes=VMEM_SMOOTH),
        name="smooth",
    )(me, *[pltpu.with_memory_space_constraint(value, pltpu.HBM) for value in (
        coeffs, weights, valid_epoch, owners, locals_, images, columns, jnp.asarray(rows))])


def add_kernel(*refs, count, groups):
    parts, outs = refs[:count], refs[count:]
    per_group = outs[0].shape[0]
    for g in range(groups):
        for i in range(per_group):
            total = parts[0][g * per_group + i].astype(F32)
            for part in parts[1:]:
                total = total + part[g * per_group + i].astype(F32)
            outs[g][i] = total.astype(BF16)


def add_and_split(parts, groups):
    blocks, block_rows, lanes = parts[0].shape
    out = jax.ShapeDtypeStruct((blocks // groups, block_rows, lanes), BF16)
    return pl.pallas_call(
        functools.partial(add_kernel, count=len(parts), groups=groups),
        in_specs=[VMEM] * len(parts), out_specs=[VMEM] * groups,
        out_shape=[out] * groups, name="add_and_split",
        compiler_params=pltpu.CompilerParams(vmem_limit_bytes=VMEM_SMALL),
    )(*parts)


def finish_kernel(*refs, tile_rows):
    parts, out_ref = refs[:-1], refs[-1]
    total = parts[0][0].astype(F32)
    for part in parts[1:]:
        total = total + part[0].astype(F32)
    for q in range(PD):
        mass = jnp.sum(total[PD * tile_rows + q:PD * tile_rows + q + 1, :], axis=1, keepdims=True)
        out_ref[q] = (total[q * tile_rows:(q + 1) * tile_rows] / (1.0 + mass)).astype(BF16)


def finish(parts, tile_rows):
    lanes = parts[0].shape[2]
    return pl.pallas_call(
        functools.partial(finish_kernel, tile_rows=tile_rows),
        in_specs=[VMEM] * len(parts), out_specs=VMEM,
        out_shape=jax.ShapeDtypeStruct((PD, tile_rows, lanes), BF16), name="finish",
        compiler_params=pltpu.CompilerParams(vmem_limit_bytes=VMEM_SMALL),
    )(*parts)


def difference_kernel(me_ref, scale_ref, owner_ref, local_ref, smooth_ref, *rest, factors, count):
    pieces, (out_ref, table_ref) = rest[:count], rest[count:]
    epoch = pl.program_id(0)

    @pl.when(epoch == 0)
    def _():
        start = 0
        for piece in pieces:
            table_ref[start:start + piece.shape[0]] = piece[...]
            start += piece.shape[0]

    scale = scale_ref[0, epoch]
    for t in range(smooth_ref.shape[1]):
        place = place_of(owner_ref[epoch, t] ^ me_ref[0], factors) * PD + local_ref[epoch, t]
        out_ref[0, t] = smooth_ref[epoch, t] - scale * table_ref[place].astype(F32)


def subtract(me, scales, owners, locals_, pieces, smoothed, factors):
    epochs, per_epoch, tile_rows, tile_side = smoothed.shape
    tile_block = pl.BlockSpec((1, per_epoch, tile_rows, tile_side), lambda e: (e, 0, 0, 0))
    patches = sum(piece.shape[0] for piece in pieces)
    return pl.pallas_call(
        functools.partial(difference_kernel, factors=factors, count=len(pieces)),
        grid=(epochs,),
        in_specs=[SMEM] * 4 + [VMEM] * (1 + len(pieces)),
        out_specs=tile_block,
        out_shape=jax.ShapeDtypeStruct(smoothed.shape, F32),
        scratch_shapes=[pltpu.VMEM((patches, tile_rows, tile_side), BF16)],
        compiler_params=pltpu.CompilerParams(
            dimension_semantics=("arbitrary",), vmem_limit_bytes=VMEM_SUBTRACT),
        name="subtract",
    )(me, scales, owners, locals_, smoothed, *pieces)


VMEM_SMOOTH = 48 * 1024 * 1024
VMEM_SMALL = 16 * 1024 * 1024
VMEM_SUBTRACT = 40 * 1024 * 1024


def body(images, coeffs, weights, scales, valid_epoch, patch_owner, patch_local):
    band_count = lax.axis_size("band")
    _, epochs, per_epoch, tile_rows, tile_side = images.shape
    factors = stage_factors(band_count)
    me = lax.axis_index("band").astype(jnp.int32).reshape(1)
    owners = patch_owner.reshape(epochs, per_epoch)
    locals_ = patch_local.reshape(epochs, per_epoch)

    smoothed, *blocks = smooth(
        me, coeffs[0].transpose(2, 0, 1), weights, valid_epoch, owners, locals_, images[0], factors, band_count)

    def exchange(value, step):
        return lax.ppermute(value, "band", [(d, d ^ step) for d in range(band_count)])

    stride = 1
    strides = []
    for k, factor in enumerate(factors):
        strides.append(stride)
        parts = [blocks[0]] + [exchange(blocks[j], j * stride) for j in range(1, factor)]
        stride *= factor
        if k + 1 < len(factors):
            blocks = add_and_split(parts, factors[k + 1])
    templates = finish(parts, tile_rows)

    pieces = [templates]
    for factor, stride in zip(reversed(factors), reversed(strides)):
        if stride > 1 and len(pieces) > 1:
            pieces = [jnp.concatenate(pieces, axis=0)]
        pieces = pieces + [exchange(piece, j * stride) for j in range(1, factor) for piece in pieces]

    difference = subtract(me, scales, owners, locals_, pieces, smoothed, factors)
    return difference[None], templates


def solution(mesh):
    return jax.shard_map(
        body,
        mesh=mesh,
        in_specs=(
            P(("groups", "band"), None, None, None, None),
            P(("groups", "band"), None, None, None),
            P(("groups", "band"), None),
            P(("groups", "band"), None),
            P(("groups", "band"), None),
            P(("groups", "band"), None, None, None),
            P(("groups", "band"), None, None),
        ),
        out_specs=(
            P(("groups", "band"), None, None, None, None),
            P(("groups", "band"), None, None),
        ),
        check_vma=False,
    )
```

```python
import functools

import jax
import jax.numpy as jnp
import numpy as np
from jax import lax
from jax.experimental import pallas as pl
from jax.experimental.pallas import tpu as pltpu
from jax.sharding import PartitionSpec as P

PD = 4
HALF = 9
P_SIZE = 3

sigmas = (0.75, 1.5, 3.0)
degrees = (4, 2, 2)

BF16 = jnp.bfloat16
F32 = jnp.float32
EXTRA = 8


def kernel_matrices(tile_side):
    place = np.arange(tile_side)
    apart = place[:, None] - place[None, :]
    offset = apart.astype(np.float32)
    inside = (np.abs(apart) <= HALF).astype(np.float32)
    taps = np.arange(-HALF, HALF + 1).astype(np.float32)
    tables = []
    for width_sigma, degree in zip(sigmas, degrees):
        scale = np.float32(2.0 * width_sigma * width_sigma)
        total = np.sum(np.exp(-taps * taps / scale), dtype=np.float32)
        envelope = np.exp(-offset * offset / scale) * inside / total
        for power in range(degree + 1):
            tables.append((envelope * (offset / np.float32(width_sigma)) ** power).astype(np.float32))
    return np.stack(tables)


def basis_pairs():
    kernel_list = []
    base_index = 0
    for degree in degrees:
        for column_power in range(degree + 1):
            for row_power in range(degree + 1 - column_power):
                kernel_list.append((base_index + row_power, base_index + column_power))
        base_index = base_index + degree + 1
    return kernel_list


def reduce_stages(band_count):
    return gather_stages(band_count)


def gather_stages(band_count):
    rest = band_count // 2
    inner = 1
    while 4 * inner * inner <= rest:
        inner *= 2
    return [factor for factor in (2, inner, rest // inner) if factor > 1]


def place_of(distance, factors):
    total = int(np.prod(factors))
    place = 0
    for factor in factors:
        total //= factor
        place = place + (distance & (factor - 1)) * total
        distance = distance >> (factor.bit_length() - 1)
    return place


def smooth_kernel(
    me_ref, weight_ref, valid_ref, owner_ref, local_ref, coef_ref, image_ref, column_ref, row_ref, spread_ref,
    smooth_ref, *rest, factors, band_count, row_count, layers,
):
    message_refs = rest[:-(2 * TOGETHER + 2)]
    total_ref, factor_ref = rest[-(2 * TOGETHER + 2):-2 * TOGETHER]
    mixer_refs, column_pass_refs = rest[-2 * TOGETHER:-TOGETHER], rest[-TOGETHER:]
    step = pl.program_id(0)
    together, per_epoch, tile_rows, tile_side = image_ref.shape
    epochs = smooth_ref.shape[0]
    depth = row_count * tile_rows

    @pl.when(step == 0)
    def _():
        total_ref[...] = jnp.zeros_like(total_ref)
        coefs = coef_ref[...].reshape(P_SIZE * epochs, coef_ref.shape[2])
        for k in range(len(layers)):
            factor_ref[k] = jnp.dot(
                coefs, spread_ref[k], precision=lax.Precision.HIGHEST, preferred_element_type=F32)

    row = lax.broadcasted_iota(jnp.int32, (tile_rows, tile_side), 0).astype(F32)
    column = lax.broadcasted_iota(jnp.int32, (tile_rows, tile_side), 1).astype(F32)
    lane = lax.broadcasted_iota(jnp.int32, (8, tile_side), 1)
    down = 2.0 * (row + 0.5) / tile_rows - 1.0

    for sub in range(together):
        epoch = step * together + sub
        mixer_ref, column_pass_ref = mixer_refs[sub], column_pass_refs[sub]

        for block in range(mixer_ref.shape[0]):
            sums = []
            for m in range(P_SIZE):
                value = None
                for k, owner in enumerate(layers):
                    if owner == block:
                        factor = factor_ref[k, pl.ds(m * epochs + epoch, 1), :]
                        term = factor * row_ref[k]
                        value = term if value is None else value + term
                sums.append(value)
            mixer_ref[block, :tile_rows] = (sums[0] + down * sums[2]).astype(BF16)
            mixer_ref[block, tile_rows:] = sums[1].astype(BF16)

        pixels = image_ref[sub].reshape(per_epoch * tile_rows, tile_side).astype(BF16)
        for c in range(0, row_count, 2):
            wide = min(2, row_count - c)
            passed = jnp.dot(
                pixels, column_ref[:, c * tile_side:(c + wide) * tile_side], preferred_element_type=F32).astype(BF16)
            for s in range(wide):
                for t in range(per_epoch):
                    column_pass_ref[t, (c + s) * tile_rows:(c + s + 1) * tile_rows] = (
                        passed[t * tile_rows:(t + 1) * tile_rows, s * tile_side:(s + 1) * tile_side])

    for sub in range(together):
        epoch = step * together + sub
        mixer_ref, column_pass_ref = mixer_refs[sub], column_pass_refs[sub]
        mixer = jnp.concatenate([mixer_ref[block] for block in range(mixer_ref.shape[0])], axis=1)[:, :depth]
        weight = jnp.full((8, tile_side), weight_ref[0, epoch] * valid_ref[0, epoch].astype(F32), F32)
        weight = weight.astype(BF16).astype(F32)
        weights = jnp.concatenate([weight] * (tile_rows // 8), axis=0)
        for first in range(0, per_epoch, 2):
            both = jnp.concatenate([column_pass_ref[first], column_pass_ref[first + 1]], axis=1)
            spatial = jnp.dot(mixer, both, preferred_element_type=F32)
            for s in range(2):
                t = first + s
                across = 2.0 * (column + (t * tile_side + 0.5)) / (per_epoch * tile_side) - 1.0
                part = spatial[:, s * tile_side:(s + 1) * tile_side]
                value = part[:tile_rows] + across * part[tile_rows:]
                smooth_ref[epoch, t] = value
                place = place_of(owner_ref[epoch, t] ^ me_ref[0], factors) * PD + local_ref[epoch, t]
                total_ref[place, :tile_rows] = (
                    total_ref[place, :tile_rows] + weights * value.astype(BF16).astype(F32))
                total_ref[place, tile_rows:] = (
                    total_ref[place, tile_rows:] + jnp.where(lane == t % tile_side, weight, 0.0))

    @pl.when(step == pl.num_programs(0) - 1)
    def _():
        groups = factors[0]
        per_group = band_count // groups
        line = lax.broadcasted_iota(jnp.int32, (8, tile_side), 0)
        part_rows = tile_rows // CHAINS
        for g in range(groups):
            @pl.loop(0, per_group)
            def _(i):
                block = (g * per_group + i) * PD
                marks = jnp.zeros((8, tile_side), F32)
                for q in range(PD):
                    for h in range(CHAINS):
                        message_refs[h * groups + g][i, q * part_rows:(q + 1) * part_rows, :] = (
                            total_ref[block + q, h * part_rows:(h + 1) * part_rows].astype(BF16))
                    marks = jnp.where(line == q, total_ref[block + q, tile_rows:], marks)
                message_refs[g][i, PD * part_rows:, :] = marks.astype(BF16)


VMEM = pl.BlockSpec(memory_space=pltpu.VMEM)
SMEM = pl.BlockSpec(memory_space=pltpu.SMEM)


def smooth(me, coeffs, weights, valid_epoch, owners, locals_, images, factors, band_count):
    epochs, per_epoch, tile_rows, tile_side = images.shape
    columns = kernel_matrices(tile_side)
    row_count = columns.shape[0]
    columns = jnp.asarray(columns.transpose(2, 0, 1).reshape(tile_side, row_count * tile_side), BF16)
    per_lanes = tile_side // tile_rows
    row_matrices = np.asarray(kernel_matrices(tile_rows), dtype=BF16).astype(np.float32)
    pairs = basis_pairs()
    layers, rows, spread = [], [], []
    for block in range(-(-row_count // per_lanes)):
        held = [[b for b, pair in enumerate(pairs) if pair[1] == block * per_lanes + i] for i in range(per_lanes)]
        for depth in range(max(map(len, held))):
            layers.append(block)
            rows.append(np.zeros((tile_rows, tile_side), np.float32))
            spread.append(np.zeros((len(pairs), tile_side), np.float32))
            for i, bases in enumerate(held):
                if depth < len(bases):
                    lanes = slice(i * tile_rows, (i + 1) * tile_rows)
                    rows[-1][:, lanes] = row_matrices[pairs[bases[depth]][0]]
                    spread[-1][bases[depth], lanes] = 1.0
    rows, spread = np.stack(rows), np.stack(spread)
    part_rows = PD * tile_rows // CHAINS
    per_group = band_count // factors[0]
    tile_block = pl.BlockSpec((TOGETHER, per_epoch, tile_rows, tile_side), lambda e: (e, 0, 0, 0))

    def whole(shape):
        return pl.BlockSpec(shape, lambda e: (0,) * len(shape), pipeline_mode=pl.Buffered(1))

    messages = [
        jax.ShapeDtypeStruct((per_group, part_rows + (EXTRA if h == 0 else 0), tile_side), BF16)
        for h in range(CHAINS) for _ in range(factors[0])]
    return pl.pallas_call(
        functools.partial(smooth_kernel, factors=factors, band_count=band_count, row_count=row_count,
            layers=layers),
        grid=(epochs // TOGETHER,),
        in_specs=[SMEM] * 5 + [
            whole(coeffs.shape), tile_block, whole(columns.shape), whole(rows.shape), whole(spread.shape)],
        out_specs=[VMEM] * (1 + len(messages)),
        out_shape=[jax.ShapeDtypeStruct(images.shape, F32)] + messages,
        scratch_shapes=[
            pltpu.VMEM((band_count * PD, tile_rows + 8, tile_side), F32),
            pltpu.VMEM((len(layers), P_SIZE * epochs, tile_side), F32),
        ] + [
            pltpu.VMEM((-(-row_count // per_lanes), 2 * tile_rows, tile_side), BF16),
        ] * TOGETHER + [
            pltpu.VMEM((per_epoch, row_count * tile_rows, tile_side), BF16),
        ] * TOGETHER,
        compiler_params=pltpu.CompilerParams(
            dimension_semantics=("arbitrary",), vmem_limit_bytes=VMEM_SMOOTH),
        name="smooth",
    )(me, *[pltpu.with_memory_space_constraint(value, pltpu.HBM) for value in (
        weights, valid_epoch, owners, locals_, coeffs, images, columns, jnp.asarray(rows), jnp.asarray(spread))])


def add_kernel(*refs, count, groups):
    parts, outs = refs[:count], refs[count:]
    per_group = outs[0].shape[0]
    for g in range(groups):
        for i in range(per_group):
            total = parts[0][g * per_group + i].astype(F32)
            for part in parts[1:]:
                total = total + part[g * per_group + i].astype(F32)
            outs[g][i] = total.astype(BF16)


def add_and_split(parts, groups):
    blocks, block_rows, lanes = parts[0].shape
    out = jax.ShapeDtypeStruct((blocks // groups, block_rows, lanes), BF16)
    return pl.pallas_call(
        functools.partial(add_kernel, count=len(parts), groups=groups),
        in_specs=[VMEM] * len(parts), out_specs=[VMEM] * groups,
        out_shape=[out] * groups, name="add_and_split",
        compiler_params=pltpu.CompilerParams(vmem_limit_bytes=VMEM_SMALL),
    )(*parts)


def finish_kernel(*refs, part_rows):
    *parts, out_ref = refs
    each = len(parts) // CHAINS
    inverse = None
    for h in range(CHAINS):
        total = parts[h * each][0].astype(F32)
        for part in parts[h * each + 1:(h + 1) * each]:
            total = total + part[0].astype(F32)
        if h == 0:
            marks = total[PD * part_rows:, :]
            inverse = jnp.broadcast_to(1.0 / (1.0 + jnp.sum(marks, axis=1, keepdims=True)), marks.shape)
        for q in range(PD):
            out_ref[q, h * part_rows:(h + 1) * part_rows] = (
                total[q * part_rows:(q + 1) * part_rows] * inverse[q:q + 1]).astype(BF16)


def finish(parts, tile_rows):
    return pl.pallas_call(
        functools.partial(finish_kernel, part_rows=tile_rows // CHAINS),
        in_specs=[VMEM] * len(parts), out_specs=VMEM,
        out_shape=jax.ShapeDtypeStruct((PD, tile_rows, parts[0].shape[2]), BF16), name="finish",
        compiler_params=pltpu.CompilerParams(vmem_limit_bytes=VMEM_SMALL),
    )(*parts)


def join_kernel(*refs):
    start = 0
    for piece in refs[:-1]:
        refs[-1][start:start + piece.shape[0]] = piece[...]
        start += piece.shape[0]


def join(pieces):
    total = sum(piece.shape[0] for piece in pieces)
    return pl.pallas_call(
        join_kernel, in_specs=[VMEM] * len(pieces), out_specs=VMEM,
        out_shape=jax.ShapeDtypeStruct((total, *pieces[0].shape[1:]), BF16), name="join",
        compiler_params=pltpu.CompilerParams(vmem_limit_bytes=VMEM_SMALL),
    )(*pieces)


def difference_kernel(me_ref, scale_ref, owner_ref, local_ref, smooth_ref, *rest, factors, count):
    pieces, (out_ref, template_ref, table_ref, ready_ref, sems) = rest[:count], rest[count:]
    epochs, per_epoch = smooth_ref.shape[:2]
    start = 0
    for piece in pieces:
        table_ref[start:start + piece.shape[0]] = piece[...]
        start += piece.shape[0]

    def copy(e):
        return pltpu.make_async_copy(ready_ref.at[e], out_ref.at[e], sems.at[e])

    for e in range(epochs):
        scale = scale_ref[0, e]
        for t in range(per_epoch):
            place = place_of(owner_ref[e, t] ^ me_ref[0], factors) * PD + local_ref[e, t]
            ready_ref[e, t] = smooth_ref[e, t] - scale * table_ref[place].astype(F32)
        if e > 0:
            copy(e - 1).start()
    template_ref[...] = table_ref[:PD]
    copy(epochs - 1).start()
    for e in range(epochs):
        copy(e).wait()


def subtract(me, scales, owners, locals_, pieces, smoothed, factors):
    tile_rows, tile_side = smoothed.shape[2:]
    own = (PD, tile_rows, tile_side)
    return pl.pallas_call(
        functools.partial(difference_kernel, factors=factors, count=len(pieces)),
        in_specs=[SMEM] * 4 + [VMEM] * (1 + len(pieces)),
        out_specs=[pl.BlockSpec(memory_space=pltpu.HBM), VMEM],
        out_shape=[jax.ShapeDtypeStruct(smoothed.shape, F32), jax.ShapeDtypeStruct(own, BF16)],
        scratch_shapes=[
            pltpu.VMEM((PD * int(np.prod(factors)), tile_rows, tile_side), BF16),
            pltpu.VMEM(smoothed.shape, F32),
            pltpu.SemaphoreType.DMA((smoothed.shape[0],)),
        ],
        compiler_params=pltpu.CompilerParams(vmem_limit_bytes=VMEM_SUBTRACT),
        name="subtract",
    )(me, scales, owners, locals_, smoothed, *pieces)


TOGETHER = 2
CHAINS = 1
VMEM_SMOOTH = 48 * 1024 * 1024
VMEM_SMALL = 16 * 1024 * 1024
VMEM_SUBTRACT = 40 * 1024 * 1024


def body(images, coeffs, weights, scales, valid_epoch, patch_owner, patch_local):
    band_count = lax.axis_size("band")
    _, epochs, per_epoch, tile_rows, tile_side = images.shape
    down, up = reduce_stages(band_count), gather_stages(band_count)
    me = lax.axis_index("band").astype(jnp.int32).reshape(1)
    owners = patch_owner.reshape(epochs, per_epoch)
    locals_ = patch_local.reshape(epochs, per_epoch)

    smoothed, *messages = smooth(
        me, coeffs[0].transpose(2, 0, 1), weights, valid_epoch, owners, locals_, images[0], down, band_count)

    def exchange(value, step):
        return lax.ppermute(value, "band", [(d, d ^ step) for d in range(band_count)])

    chains = [messages[h * down[0]:(h + 1) * down[0]] for h in range(CHAINS)]
    stride = 1
    for k, factor in enumerate(down):
        for h in range(CHAINS):
            blocks = chains[h]
            parts = [blocks[0]] + [exchange(blocks[j], j * stride) for j in range(1, factor)]
            chains[h] = add_and_split(parts, down[k + 1]) if k + 1 < len(down) else parts
        stride *= factor

    pieces = [finish([part for chain in chains for part in chain], tile_rows)]
    stride = band_count
    for factor in reversed(up):
        stride //= factor
        if len(pieces) > 2:
            pieces = [join(pieces)]
        pieces = pieces + [exchange(piece, j * stride) for j in range(1, factor) for piece in pieces]

    difference, templates = subtract(me, scales, owners, locals_, pieces, smoothed, up)
    return difference[None], templates


def solution(mesh):
    return jax.shard_map(
        body,
        mesh=mesh,
        in_specs=(
            P(("groups", "band"), None, None, None, None),
            P(("groups", "band"), None, None, None),
            P(("groups", "band"), None),
            P(("groups", "band"), None),
            P(("groups", "band"), None),
            P(("groups", "band"), None, None, None),
            P(("groups", "band"), None, None),
        ),
        out_specs=(
            P(("groups", "band"), None, None, None, None),
            P(("groups", "band"), None, None),
        ),
        check_vma=False,
    )
```

```python
import functools

import jax
import jax.numpy as jnp
import numpy as np
from jax import lax
from jax.experimental import pallas as pl
from jax.experimental.pallas import tpu as pltpu
from jax.sharding import PartitionSpec as P


PD = 4
HALF = 9
P_SIZE = 3

sigmas = (0.75, 1.5, 3.0)
degrees = (4, 2, 2)

BF16 = jnp.bfloat16
F32 = jnp.float32
EXTRA = 8


def kernel_matrices(tile_side):
    place = np.arange(tile_side)
    apart = place[:, None] - place[None, :]
    offset = apart.astype(np.float32)
    inside = (np.abs(apart) <= HALF).astype(np.float32)
    taps = np.arange(-HALF, HALF + 1).astype(np.float32)
    tables = []
    for width_sigma, degree in zip(sigmas, degrees):
        scale = np.float32(2.0 * width_sigma * width_sigma)
        total = np.sum(np.exp(-taps * taps / scale), dtype=np.float32)
        envelope = np.exp(-offset * offset / scale) * inside / total
        for power in range(degree + 1):
            tables.append((envelope * (offset / np.float32(width_sigma)) ** power).astype(np.float32))
    return np.stack(tables)


def basis_pairs():
    kernel_list = []
    base_index = 0
    for degree in degrees:
        for column_power in range(degree + 1):
            for row_power in range(degree + 1 - column_power):
                kernel_list.append((base_index + row_power, base_index + column_power))
        base_index = base_index + degree + 1
    return kernel_list


def reduce_stages(band_count):
    return gather_stages(band_count)


def gather_stages(band_count):
    rest = band_count // 2
    inner = 1
    while 4 * inner * inner <= rest:
        inner *= 2
    return [factor for factor in (2, inner, rest // inner) if factor > 1]


def place_of(distance, factors):
    total = int(np.prod(factors))
    place = 0
    for factor in factors:
        total //= factor
        place = place + (distance & (factor - 1)) * total
        distance = distance >> (factor.bit_length() - 1)
    return place


def smooth_kernel(
    me_ref, weight_hbm, valid_hbm, owner_hbm, local_hbm, coef_hbm, spread_hbm, column_hbm, row_hbm, image_hbm,
    smooth_ref, *rest, factors, band_count, row_count, layers,
):
    message_refs, rest = rest[:factors[0]], rest[factors[0]:]
    weight_ref, valid_ref, owner_ref, local_ref, coef_ref, spread_ref, column_ref, row_ref, held_ref = rest[:9]
    small_sems, image_sems, total_ref, factor_ref = rest[9:13]
    mixer_refs, column_pass_refs = rest[13:13 + 2 * TOGETHER], rest[13 + 2 * TOGETHER:]
    epochs, per_epoch, tile_rows, tile_side = smooth_ref.shape
    depth = row_count * tile_rows

    small = [pltpu.make_async_copy(source, target, small_sems.at[k]) for k, (source, target) in enumerate((
        (coef_hbm, coef_ref), (spread_hbm, spread_ref), (row_hbm, row_ref), (column_hbm, column_ref),
        (weight_hbm, weight_ref), (valid_hbm, valid_ref), (owner_hbm, owner_ref), (local_hbm, local_ref)))]
    images = [
        pltpu.make_async_copy(image_hbm.at[epoch], held_ref.at[epoch], image_sems.at[epoch])
        for epoch in range(epochs)]
    for copy in small[:4] + images[:TOGETHER] + small[4:] + images[TOGETHER:]:
        copy.start()

    total_ref[...] = jnp.zeros_like(total_ref)
    small[0].wait()
    small[1].wait()
    left = coef_ref[...].reshape(P_SIZE * epochs, coef_ref.shape[2])
    spread_coefs = None
    for _ in range(3):
        piece = left.astype(BF16)
        left = left - piece.astype(F32)
        term = jnp.dot(piece, spread_ref[...], preferred_element_type=F32)
        spread_coefs = term if spread_coefs is None else spread_coefs + term
    for k in range(len(layers)):
        factor_ref[k] = spread_coefs[:, k * tile_side:(k + 1) * tile_side]
    for copy in small[2:]:
        copy.wait()

    row = lax.broadcasted_iota(jnp.int32, (tile_rows, tile_side), 0).astype(F32)
    column = lax.broadcasted_iota(jnp.int32, (tile_rows, tile_side), 1).astype(F32)
    lane = lax.broadcasted_iota(jnp.int32, (8, tile_side), 1)
    down = 2.0 * (row + 0.5) / tile_rows - 1.0

    def mixers(epoch, mixer_ref):
        for block in range(mixer_ref.shape[0]):
            sums = []
            for m in range(P_SIZE):
                value = None
                for k, owner in enumerate(layers):
                    if owner == block:
                        factor = factor_ref[k, m * epochs + epoch:m * epochs + epoch + 1, :]
                        term = factor * row_ref[k]
                        value = term if value is None else value + term
                sums.append(value)
            mixer_ref[block, :tile_rows] = (sums[0] + down * sums[2]).astype(BF16)
            mixer_ref[block, tile_rows:] = sums[1].astype(BF16)

    def column_pass(epoch, column_pass_ref):
        pixels = held_ref[epoch].reshape(per_epoch * tile_rows, tile_side).astype(BF16)
        for c in range(0, row_count, 2):
            wide = min(2, row_count - c)
            passed = jnp.dot(
                pixels, column_ref[:, c * tile_side:(c + wide) * tile_side], preferred_element_type=F32).astype(BF16)
            for s in range(wide):
                for t in range(per_epoch):
                    column_pass_ref[t, (c + s) * tile_rows:(c + s + 1) * tile_rows] = (
                        passed[t * tile_rows:(t + 1) * tile_rows, s * tile_side:(s + 1) * tile_side])

    def row_pass(epoch, mixer_ref, column_pass_ref):
        mixer = jnp.concatenate([mixer_ref[block] for block in range(mixer_ref.shape[0])], axis=1)[:, :depth]
        weight = jnp.full((8, tile_side), weight_ref[0, epoch] * valid_ref[0, epoch].astype(F32), F32)
        weight = weight.astype(BF16).astype(F32)
        weights = jnp.concatenate([weight] * (tile_rows // 8), axis=0)
        for first in range(0, per_epoch, 2):
            both = jnp.concatenate([column_pass_ref[first], column_pass_ref[first + 1]], axis=1)
            spatial = jnp.dot(mixer, both, preferred_element_type=F32)
            for s in range(2):
                t = first + s
                across = 2.0 * (column + (t * tile_side + 0.5)) / (per_epoch * tile_side) - 1.0
                part = spatial[:, s * tile_side:(s + 1) * tile_side]
                value = part[:tile_rows] + across * part[tile_rows:]
                smooth_ref[epoch, t] = value
                place = place_of(owner_ref[epoch, t] ^ me_ref[0], factors) * PD + local_ref[epoch, t]
                total_ref[place, :tile_rows] = (
                    total_ref[place, :tile_rows] + weights * value.astype(BF16).astype(F32))
                total_ref[place, tile_rows:] = (
                    total_ref[place, tile_rows:] + jnp.where(lane == t % tile_side, weight, 0.0))

    for step in range(epochs // TOGETHER + 1):
        now = range(step * TOGETHER, min(epochs, (step + 1) * TOGETHER))
        for epoch in now:
            images[epoch].wait()
        before = range((step - 1) * TOGETHER, step * TOGETHER) if step else ()
        for k in range(TOGETHER):
            for epoch in now[k:k + 1]:
                column_pass(epoch, column_pass_refs[epoch % (2 * TOGETHER)])
                mixers(epoch, mixer_refs[epoch % (2 * TOGETHER)])
            for epoch in before[k:k + 1]:
                slot = epoch % (2 * TOGETHER)
                row_pass(epoch, mixer_refs[slot], column_pass_refs[slot])

    per_group = band_count // factors[0]
    line = lax.broadcasted_iota(jnp.int32, (8, tile_side), 0)
    for g in range(factors[0]):
        @pl.loop(0, per_group)
        def _(i):
            block = (g * per_group + i) * PD
            marks = jnp.zeros((8, tile_side), F32)
            for q in range(PD):
                message_refs[g][i, q * tile_rows:(q + 1) * tile_rows, :] = (
                    total_ref[block + q, :tile_rows].astype(BF16))
                marks = jnp.where(line == q, total_ref[block + q, tile_rows:], marks)
            message_refs[g][i, PD * tile_rows:, :] = marks.astype(BF16)


VMEM = pl.BlockSpec(memory_space=pltpu.VMEM)
SMEM = pl.BlockSpec(memory_space=pltpu.SMEM)


def smooth(me, coeffs, weights, valid_epoch, owners, locals_, images, factors, band_count):
    epochs, per_epoch, tile_rows, tile_side = images.shape
    columns = kernel_matrices(tile_side)
    row_count = columns.shape[0]
    columns = jnp.asarray(columns.transpose(2, 0, 1).reshape(tile_side, row_count * tile_side), BF16)
    per_lanes = tile_side // tile_rows
    row_matrices = np.asarray(kernel_matrices(tile_rows), dtype=BF16).astype(np.float32)
    pairs = basis_pairs()
    layers, rows, spread = [], [], []
    for block in range(-(-row_count // per_lanes)):
        held = [[b for b, pair in enumerate(pairs) if pair[1] == block * per_lanes + i] for i in range(per_lanes)]
        for depth in range(max(map(len, held))):
            layers.append(block)
            rows.append(np.zeros((tile_rows, tile_side), np.float32))
            spread.append(np.zeros((len(pairs), tile_side), np.float32))
            for i, bases in enumerate(held):
                if depth < len(bases):
                    lanes = slice(i * tile_rows, (i + 1) * tile_rows)
                    rows[-1][:, lanes] = row_matrices[pairs[bases[depth]][0]]
                    spread[-1][bases[depth], lanes] = 1.0
    rows = jnp.asarray(np.stack(rows))
    spread = jnp.asarray(np.concatenate(spread, axis=1), BF16)
    block_rows = PD * tile_rows + EXTRA
    per_group = band_count // factors[0]
    messages = [jax.ShapeDtypeStruct((per_group, block_rows, tile_side), BF16)] * factors[0]
    return pl.pallas_call(
        functools.partial(smooth_kernel, factors=factors, band_count=band_count, row_count=row_count,
            layers=layers),
        in_specs=[SMEM] + [pl.BlockSpec(memory_space=pltpu.HBM)] * 9,
        out_specs=[VMEM] * (1 + len(messages)),
        out_shape=[jax.ShapeDtypeStruct(images.shape, F32)] + messages,
        scratch_shapes=[
            *(pltpu.SMEM(value.shape, value.dtype) for value in (weights, valid_epoch, owners, locals_)),
            *(pltpu.VMEM(value.shape, value.dtype) for value in (coeffs, spread, columns, rows, images)),
            pltpu.SemaphoreType.DMA((8,)),
            pltpu.SemaphoreType.DMA((epochs,)),
            pltpu.VMEM((band_count * PD, tile_rows + 8, tile_side), F32),
            pltpu.VMEM((len(layers), P_SIZE * epochs, tile_side), F32),
        ] + [
            pltpu.VMEM((-(-row_count // per_lanes), 2 * tile_rows, tile_side), BF16),
        ] * (2 * TOGETHER) + [
            pltpu.VMEM((per_epoch, row_count * tile_rows, tile_side), BF16),
        ] * (2 * TOGETHER),
        compiler_params=pltpu.CompilerParams(vmem_limit_bytes=VMEM_SMOOTH),
        name="smooth",
    )(me, *[pltpu.with_memory_space_constraint(value, pltpu.HBM) for value in (
        weights, valid_epoch, owners, locals_, coeffs, spread, columns, rows, images)])


def add_kernel(*refs, count, groups):
    parts, outs = refs[:count], refs[count:]
    per_group = outs[0].shape[0]
    for g in range(groups):
        for i in range(per_group):
            total = parts[0][g * per_group + i].astype(F32)
            for part in parts[1:]:
                total = total + part[g * per_group + i].astype(F32)
            outs[g][i] = total.astype(BF16)


def add_and_split(parts, groups):
    blocks, block_rows, lanes = parts[0].shape
    out = jax.ShapeDtypeStruct((blocks // groups, block_rows, lanes), BF16)
    return pl.pallas_call(
        functools.partial(add_kernel, count=len(parts), groups=groups),
        in_specs=[VMEM] * len(parts), out_specs=[VMEM] * groups,
        out_shape=[out] * groups, name="add_and_split",
        compiler_params=pltpu.CompilerParams(vmem_limit_bytes=VMEM_SMALL),
    )(*parts)


def finish_kernel(*refs):
    *parts, out_ref = refs
    tile_rows = out_ref.shape[1]
    total = parts[0][0].astype(F32)
    for part in parts[1:]:
        total = total + part[0].astype(F32)
    marks = total[PD * tile_rows:, :]
    inverse = jnp.broadcast_to(1.0 / (1.0 + jnp.sum(marks, axis=1, keepdims=True)), marks.shape)
    for q in range(PD):
        out_ref[q] = (total[q * tile_rows:(q + 1) * tile_rows] * inverse[q:q + 1]).astype(BF16)


def finish(parts, tile_rows):
    return pl.pallas_call(
        finish_kernel, in_specs=[VMEM] * len(parts), out_specs=VMEM,
        out_shape=jax.ShapeDtypeStruct((PD, tile_rows, parts[0].shape[2]), BF16), name="finish",
        compiler_params=pltpu.CompilerParams(vmem_limit_bytes=VMEM_SMALL),
    )(*parts)


def join_kernel(*refs):
    start = 0
    for piece in refs[:-1]:
        refs[-1][start:start + piece.shape[0]] = piece[...]
        start += piece.shape[0]


def join(pieces):
    total = sum(piece.shape[0] for piece in pieces)
    return pl.pallas_call(
        join_kernel, in_specs=[VMEM] * len(pieces), out_specs=VMEM,
        out_shape=jax.ShapeDtypeStruct((total, *pieces[0].shape[1:]), BF16), name="join",
        compiler_params=pltpu.CompilerParams(vmem_limit_bytes=VMEM_SMALL),
    )(*pieces)


def difference_kernel(me_ref, scale_ref, owner_ref, local_ref, smooth_ref, *rest, factors, count):
    pieces, (out_ref, template_ref, table_ref, ready_ref, sems) = rest[:count], rest[count:]
    epochs, per_epoch = smooth_ref.shape[:2]
    start = 0
    for piece in pieces:
        table_ref[start:start + piece.shape[0]] = piece[...]
        start += piece.shape[0]

    def copy(e):
        return pltpu.make_async_copy(ready_ref.at[e], out_ref.at[e], sems.at[e])

    for e in range(epochs):
        scale = scale_ref[0, e]
        for t in range(per_epoch):
            place = place_of(owner_ref[e, t] ^ me_ref[0], factors) * PD + local_ref[e, t]
            ready_ref[e, t] = smooth_ref[e, t] - scale * table_ref[place].astype(F32)
        if e > 0:
            copy(e - 1).start()
    template_ref[...] = table_ref[:PD]
    copy(epochs - 1).start()
    for e in range(epochs):
        copy(e).wait()


def subtract(me, scales, owners, locals_, pieces, smoothed, factors):
    tile_rows, tile_side = smoothed.shape[2:]
    own = (PD, tile_rows, tile_side)
    return pl.pallas_call(
        functools.partial(difference_kernel, factors=factors, count=len(pieces)),
        in_specs=[SMEM] * 4 + [VMEM] * (1 + len(pieces)),
        out_specs=[pl.BlockSpec(memory_space=pltpu.HBM), VMEM],
        out_shape=[jax.ShapeDtypeStruct(smoothed.shape, F32), jax.ShapeDtypeStruct(own, BF16)],
        scratch_shapes=[
            pltpu.VMEM((PD * int(np.prod(factors)), tile_rows, tile_side), BF16),
            pltpu.VMEM(smoothed.shape, F32),
            pltpu.SemaphoreType.DMA((smoothed.shape[0],)),
        ],
        compiler_params=pltpu.CompilerParams(vmem_limit_bytes=VMEM_SUBTRACT),
        name="subtract",
    )(me, scales, owners, locals_, smoothed, *pieces)


TOGETHER = 2
VMEM_SMOOTH = 48 * 1024 * 1024
VMEM_SMALL = 16 * 1024 * 1024
VMEM_SUBTRACT = 40 * 1024 * 1024


def body(images, coeffs, weights, scales, valid_epoch, patch_owner, patch_local):
    band_count = lax.axis_size("band")
    _, epochs, per_epoch, tile_rows, _ = images.shape
    down, up = reduce_stages(band_count), gather_stages(band_count)
    me = lax.axis_index("band").astype(jnp.int32).reshape(1)
    owners = patch_owner.reshape(epochs, per_epoch)
    locals_ = patch_local.reshape(epochs, per_epoch)

    smoothed, *messages = smooth(
        me, coeffs[0].transpose(2, 0, 1), weights, valid_epoch, owners, locals_, images[0], down, band_count)

    def exchange(value, step):
        return lax.ppermute(value, "band", [(d, d ^ step) for d in range(band_count)])

    first, second, third = down
    half = third // 2
    parts = [messages[0]] + [exchange(messages[j], j) for j in range(1, first)]
    split = add_and_split(parts, 2 * second)
    near, far = split[0::2], split[1::2]
    far = [far[0]] + [exchange(far[j], j * first) for j in range(1, second)]
    near = [near[0]] + [exchange(near[j], j * first) for j in range(1, second)]
    stride = first * second
    far = add_and_split(far, third - half)
    arrived = [exchange(far[j - half], j * stride) for j in reversed(range(half, third))]
    near = add_and_split(near, half)
    arrived = [near[0]] + [exchange(near[j], j * stride) for j in range(1, half)] + arrived

    pieces = [finish(arrived, tile_rows)]
    own = pieces[0]
    distant = [exchange(own, j * stride) for j in reversed(range(half, third))][::-1]
    close = [own] + [exchange(own, j * stride) for j in range(1, half)]
    halves = [join(close) if len(close) > 1 else close[0], join(distant) if len(distant) > 1 else distant[0]]
    pieces = []
    for piece in halves:
        pieces.append([piece] + [exchange(piece, j * first) for j in range(1, second)])
    pieces = [piece for pair in zip(*pieces) for piece in pair]
    pieces = pieces + [exchange(piece, j) for j in range(1, first) for piece in pieces]

    difference, templates = subtract(me, scales, owners, locals_, pieces, smoothed, up)
    return difference[None], templates


def solution(mesh):
    return jax.shard_map(
        body,
        mesh=mesh,
        in_specs=(
            P(("groups", "band"), None, None, None, None),
            P(("groups", "band"), None, None, None),
            P(("groups", "band"), None),
            P(("groups", "band"), None),
            P(("groups", "band"), None),
            P(("groups", "band"), None, None, None),
            P(("groups", "band"), None, None),
        ),
        out_specs=(
            P(("groups", "band"), None, None, None, None),
            P(("groups", "band"), None, None),
        ),
        check_vma=False,
    )
```

```python
import functools

import jax
import jax.numpy as jnp
import numpy as np
from jax import lax
from jax.experimental import pallas as pl
from jax.experimental.pallas import tpu as pltpu
from jax.sharding import PartitionSpec as P


PD = 4
HALF = 9
P_SIZE = 3

sigmas = (0.75, 1.5, 3.0)
degrees = (4, 2, 2)

BF16 = jnp.bfloat16
F32 = jnp.float32
EXTRA = 8


def kernel_matrices(tile_side):
    place = np.arange(tile_side)
    apart = place[:, None] - place[None, :]
    offset = apart.astype(np.float32)
    inside = (np.abs(apart) <= HALF).astype(np.float32)
    taps = np.arange(-HALF, HALF + 1).astype(np.float32)
    tables = []
    for width_sigma, degree in zip(sigmas, degrees):
        scale = np.float32(2.0 * width_sigma * width_sigma)
        total = np.sum(np.exp(-taps * taps / scale), dtype=np.float32)
        envelope = np.exp(-offset * offset / scale) * inside / total
        for power in range(degree + 1):
            tables.append((envelope * (offset / np.float32(width_sigma)) ** power).astype(np.float32))
    return np.stack(tables)


def basis_pairs():
    kernel_list = []
    base_index = 0
    for degree in degrees:
        for column_power in range(degree + 1):
            for row_power in range(degree + 1 - column_power):
                kernel_list.append((base_index + row_power, base_index + column_power))
        base_index = base_index + degree + 1
    return kernel_list


def gather_stages(band_count):
    rest = band_count // 2
    inner = 1
    while 4 * inner * inner <= rest:
        inner *= 2
    return [factor for factor in (2, inner, rest // inner) if factor > 1]


def place_of(distance, factors):
    total = int(np.prod(factors))
    place = 0
    for factor in factors:
        total //= factor
        place = place + (distance & (factor - 1)) * total
        distance = distance >> (factor.bit_length() - 1)
    return place


def send_groups(third):
    half = third // 2
    if third > 4:
        return [(half, third), (0, half)]
    return [(digit, digit + 1) for digit in reversed(range(half, third))] + [(0, half)]


def send_place(distance, stages):
    first, second, third = stages
    over = distance >> (first.bit_length() - 1)
    along = over >> (second.bit_length() - 1)
    return ((distance & (first - 1)) * third + along) * second + (over & (second - 1))


def smooth_kernel(
    me_ref, weight_hbm, valid_hbm, owner_hbm, local_hbm, coef_hbm, spread_hbm, column_hbm, row_hbm, image_hbm,
    smooth_ref, *rest, factors, row_count, layers,
):
    first, second, third = factors
    starts = [(core * third + low) * second for core in range(first) for low, high in send_groups(third)]
    message_refs, rest = rest[:len(starts)], rest[len(starts):]
    weight_ref, valid_ref, owner_ref, local_ref, coef_ref, spread_ref, column_ref, row_ref, held_ref = rest[:9]
    small_sems, image_sems, total_ref, factor_ref = rest[9:13]
    mixer_refs, column_pass_refs = rest[13:13 + 2 * TOGETHER], rest[13 + 2 * TOGETHER:]
    epochs, per_epoch, tile_rows, tile_side = smooth_ref.shape
    depth = row_count * tile_rows

    small = [pltpu.make_async_copy(source, target, small_sems.at[k]) for k, (source, target) in enumerate((
        (coef_hbm, coef_ref), (spread_hbm, spread_ref), (row_hbm, row_ref), (column_hbm, column_ref),
        (weight_hbm, weight_ref), (valid_hbm, valid_ref), (owner_hbm, owner_ref), (local_hbm, local_ref)))]
    images = [
        pltpu.make_async_copy(image_hbm.at[epoch], held_ref.at[epoch], image_sems.at[epoch])
        for epoch in range(epochs)]
    for copy in small[:4] + images[:TOGETHER] + small[4:] + images[TOGETHER:]:
        copy.start()

    total_ref[...] = jnp.zeros_like(total_ref)
    small[0].wait()
    small[1].wait()
    left = coef_ref[...].reshape(P_SIZE * epochs, coef_ref.shape[2])
    spread_coefs = None
    for _ in range(3):
        piece = left.astype(BF16)
        left = left - piece.astype(F32)
        term = jnp.dot(piece, spread_ref[...], preferred_element_type=F32)
        spread_coefs = term if spread_coefs is None else spread_coefs + term
    for k in range(len(layers)):
        factor_ref[k] = spread_coefs[:, k * tile_side:(k + 1) * tile_side]
    for copy in small[2:]:
        copy.wait()

    row = lax.broadcasted_iota(jnp.int32, (tile_rows, tile_side), 0).astype(F32)
    column = lax.broadcasted_iota(jnp.int32, (tile_rows, tile_side), 1).astype(F32)
    lane = lax.broadcasted_iota(jnp.int32, (8, tile_side), 1)
    down = 2.0 * (row + 0.5) / tile_rows - 1.0

    def mixers(epoch, mixer_ref):
        for block in range(mixer_ref.shape[0]):
            sums = []
            for m in range(P_SIZE):
                value = None
                for k, owner in enumerate(layers):
                    if owner == block:
                        factor = factor_ref[k, m * epochs + epoch:m * epochs + epoch + 1, :]
                        term = factor * row_ref[k]
                        value = term if value is None else value + term
                sums.append(value)
            mixer_ref[block, :tile_rows] = (sums[0] + down * sums[2]).astype(BF16)
            mixer_ref[block, tile_rows:] = sums[1].astype(BF16)

    def column_pass(epoch, column_pass_ref):
        pixels = held_ref[epoch].reshape(per_epoch * tile_rows, tile_side).astype(BF16)
        for c in range(0, row_count, 2):
            wide = min(2, row_count - c)
            passed = jnp.dot(
                pixels, column_ref[:, c * tile_side:(c + wide) * tile_side], preferred_element_type=F32).astype(BF16)
            for s in range(wide):
                for t in range(per_epoch):
                    column_pass_ref[t, (c + s) * tile_rows:(c + s + 1) * tile_rows] = (
                        passed[t * tile_rows:(t + 1) * tile_rows, s * tile_side:(s + 1) * tile_side])

    def row_pass(epoch, mixer_ref, column_pass_ref):
        mixer = jnp.concatenate([mixer_ref[block] for block in range(mixer_ref.shape[0])], axis=1)[:, :depth]
        weight = jnp.full((8, tile_side), weight_ref[0, epoch] * valid_ref[0, epoch].astype(F32), F32)
        weight = weight.astype(BF16).astype(F32)
        weights = jnp.concatenate([weight] * (tile_rows // 8), axis=0)
        for left in range(0, per_epoch, 2):
            both = jnp.concatenate([column_pass_ref[left], column_pass_ref[left + 1]], axis=1)
            spatial = jnp.dot(mixer, both, preferred_element_type=F32)
            for s in range(2):
                t = left + s
                across = 2.0 * (column + (t * tile_side + 0.5)) / (per_epoch * tile_side) - 1.0
                part = spatial[:, s * tile_side:(s + 1) * tile_side]
                value = part[:tile_rows] + across * part[tile_rows:]
                smooth_ref[epoch, t] = value
                place = send_place(owner_ref[epoch, t] ^ me_ref[0], factors) * PD + local_ref[epoch, t]
                total_ref[place, :tile_rows] = (
                    total_ref[place, :tile_rows] + weights * value.astype(BF16).astype(F32))
                total_ref[place, tile_rows:] = (
                    total_ref[place, tile_rows:] + jnp.where(lane == t % tile_side, weight, 0.0))

    for step in range(epochs // TOGETHER + 1):
        now = range(step * TOGETHER, min(epochs, (step + 1) * TOGETHER))
        for epoch in now:
            images[epoch].wait()
        before = range((step - 1) * TOGETHER, step * TOGETHER) if step else ()
        for k in range(TOGETHER):
            for epoch in now[k:k + 1]:
                column_pass(epoch, column_pass_refs[epoch % (2 * TOGETHER)])
                mixers(epoch, mixer_refs[epoch % (2 * TOGETHER)])
            for epoch in before[k:k + 1]:
                slot = epoch % (2 * TOGETHER)
                row_pass(epoch, mixer_refs[slot], column_pass_refs[slot])

    line = lax.broadcasted_iota(jnp.int32, (8, tile_side), 0)
    for start, message_ref in zip(starts, message_refs):
        @pl.loop(0, message_ref.shape[0])
        def _(i):
            block = (start + i) * PD
            marks = jnp.zeros((8, tile_side), F32)
            for q in range(PD):
                message_ref[i, q * tile_rows:(q + 1) * tile_rows, :] = (
                    total_ref[block + q, :tile_rows].astype(BF16))
                marks = jnp.where(line == q, total_ref[block + q, tile_rows:], marks)
            message_ref[i, PD * tile_rows:, :] = marks.astype(BF16)


VMEM = pl.BlockSpec(memory_space=pltpu.VMEM)
SMEM = pl.BlockSpec(memory_space=pltpu.SMEM)


def smooth(me, coeffs, weights, valid_epoch, owners, locals_, images, factors, band_count):
    epochs, per_epoch, tile_rows, tile_side = images.shape
    columns = kernel_matrices(tile_side)
    row_count = columns.shape[0]
    columns = jnp.asarray(columns.transpose(2, 0, 1).reshape(tile_side, row_count * tile_side), BF16)
    per_lanes = tile_side // tile_rows
    row_matrices = np.asarray(kernel_matrices(tile_rows), dtype=BF16).astype(np.float32)
    pairs = basis_pairs()
    layers, rows, spread = [], [], []
    for block in range(-(-row_count // per_lanes)):
        held = [[b for b, pair in enumerate(pairs) if pair[1] == block * per_lanes + i] for i in range(per_lanes)]
        for depth in range(max(map(len, held))):
            layers.append(block)
            rows.append(np.zeros((tile_rows, tile_side), np.float32))
            spread.append(np.zeros((len(pairs), tile_side), np.float32))
            for i, bases in enumerate(held):
                if depth < len(bases):
                    lanes = slice(i * tile_rows, (i + 1) * tile_rows)
                    rows[-1][:, lanes] = row_matrices[pairs[bases[depth]][0]]
                    spread[-1][bases[depth], lanes] = 1.0
    rows = jnp.asarray(np.stack(rows))
    spread = jnp.asarray(np.concatenate(spread, axis=1), BF16)
    block_rows = PD * tile_rows + EXTRA
    first, second, third = factors
    messages = [
        jax.ShapeDtypeStruct(((high - low) * second, block_rows, tile_side), BF16)
        for _ in range(first) for low, high in send_groups(third)]
    return pl.pallas_call(
        functools.partial(smooth_kernel, factors=factors, row_count=row_count,
            layers=layers),
        in_specs=[SMEM] + [pl.BlockSpec(memory_space=pltpu.HBM)] * 9,
        out_specs=[VMEM] * (1 + len(messages)),
        out_shape=[jax.ShapeDtypeStruct(images.shape, F32)] + messages,
        scratch_shapes=[
            *(pltpu.SMEM(value.shape, value.dtype) for value in (weights, valid_epoch, owners, locals_)),
            *(pltpu.VMEM(value.shape, value.dtype) for value in (coeffs, spread, columns, rows, images)),
            pltpu.SemaphoreType.DMA((8,)),
            pltpu.SemaphoreType.DMA((epochs,)),
            pltpu.VMEM((band_count * PD, tile_rows + 8, tile_side), F32),
            pltpu.VMEM((len(layers), P_SIZE * epochs, tile_side), F32),
        ] + [
            pltpu.VMEM((-(-row_count // per_lanes), 2 * tile_rows, tile_side), BF16),
        ] * (2 * TOGETHER) + [
            pltpu.VMEM((per_epoch, row_count * tile_rows, tile_side), BF16),
        ] * (2 * TOGETHER),
        compiler_params=pltpu.CompilerParams(vmem_limit_bytes=VMEM_SMOOTH),
        name="smooth",
    )(me, *[pltpu.with_memory_space_constraint(value, pltpu.HBM) for value in (
        weights, valid_epoch, owners, locals_, coeffs, spread, columns, rows, images)])


def add_kernel(*refs, count, groups, minor):
    parts, outs = refs[:count], refs[count:]
    per_group = outs[0].shape[0]
    for g in range(groups):
        for i in range(per_group):
            place = i * groups + g if minor else g * per_group + i
            total = parts[0][place].astype(F32)
            for part in parts[1:]:
                total = total + part[place].astype(F32)
            outs[g][i] = total.astype(BF16)


def add_and_split(parts, groups, minor=False):
    blocks, block_rows, lanes = parts[0].shape
    out = jax.ShapeDtypeStruct((blocks // groups, block_rows, lanes), BF16)
    return pl.pallas_call(
        functools.partial(add_kernel, count=len(parts), groups=groups, minor=minor),
        in_specs=[VMEM] * len(parts), out_specs=[VMEM] * groups,
        out_shape=[out] * groups, name="add_and_split",
        compiler_params=pltpu.CompilerParams(vmem_limit_bytes=VMEM_SMALL),
    )(*parts)


def finish_kernel(*refs):
    *parts, out_ref = refs
    tile_rows = out_ref.shape[1]
    total = parts[0][0].astype(F32)
    for part in parts[1:]:
        total = total + part[0].astype(F32)
    marks = total[PD * tile_rows:, :]
    inverse = jnp.broadcast_to(1.0 / (1.0 + jnp.sum(marks, axis=1, keepdims=True)), marks.shape)
    for q in range(PD):
        out_ref[q] = (total[q * tile_rows:(q + 1) * tile_rows] * inverse[q:q + 1]).astype(BF16)


def finish(parts, tile_rows):
    return pl.pallas_call(
        finish_kernel, in_specs=[VMEM] * len(parts), out_specs=VMEM,
        out_shape=jax.ShapeDtypeStruct((PD, tile_rows, parts[0].shape[2]), BF16), name="finish",
        compiler_params=pltpu.CompilerParams(vmem_limit_bytes=VMEM_SMALL),
    )(*parts)


def join_kernel(*refs):
    start = 0
    for piece in refs[:-1]:
        refs[-1][start:start + piece.shape[0]] = piece[...]
        start += piece.shape[0]


def join(pieces):
    total = sum(piece.shape[0] for piece in pieces)
    return pl.pallas_call(
        join_kernel, in_specs=[VMEM] * len(pieces), out_specs=VMEM,
        out_shape=jax.ShapeDtypeStruct((total, *pieces[0].shape[1:]), BF16), name="join",
        compiler_params=pltpu.CompilerParams(vmem_limit_bytes=VMEM_SMALL),
    )(*pieces)


def difference_kernel(me_ref, scale_ref, owner_ref, local_ref, smooth_ref, *rest, factors, count):
    pieces, (out_ref, template_ref, table_ref, ready_ref, sems) = rest[:count], rest[count:]
    epochs, per_epoch = smooth_ref.shape[:2]
    start = 0
    for piece in pieces:
        table_ref[start:start + piece.shape[0]] = piece[...]
        start += piece.shape[0]

    def copy(e):
        return pltpu.make_async_copy(ready_ref.at[e], out_ref.at[e], sems.at[e])

    for e in range(epochs):
        scale = scale_ref[0, e]
        for t in range(per_epoch):
            place = place_of(owner_ref[e, t] ^ me_ref[0], factors) * PD + local_ref[e, t]
            ready_ref[e, t] = smooth_ref[e, t] - scale * table_ref[place].astype(F32)
        if e > 0:
            copy(e - 1).start()
    template_ref[...] = table_ref[:PD]
    copy(epochs - 1).start()
    for e in range(epochs):
        copy(e).wait()


def subtract(me, scales, owners, locals_, pieces, smoothed, factors):
    tile_rows, tile_side = smoothed.shape[2:]
    own = (PD, tile_rows, tile_side)
    return pl.pallas_call(
        functools.partial(difference_kernel, factors=factors, count=len(pieces)),
        in_specs=[SMEM] * 4 + [VMEM] * (1 + len(pieces)),
        out_specs=[pl.BlockSpec(memory_space=pltpu.HBM), VMEM],
        out_shape=[jax.ShapeDtypeStruct(smoothed.shape, F32), jax.ShapeDtypeStruct(own, BF16)],
        scratch_shapes=[
            pltpu.VMEM((PD * int(np.prod(factors)), tile_rows, tile_side), BF16),
            pltpu.VMEM(smoothed.shape, F32),
            pltpu.SemaphoreType.DMA((smoothed.shape[0],)),
        ],
        compiler_params=pltpu.CompilerParams(vmem_limit_bytes=VMEM_SUBTRACT),
        name="subtract",
    )(me, scales, owners, locals_, smoothed, *pieces)


TOGETHER = 2
VMEM_SMOOTH = 48 * 1024 * 1024
VMEM_SMALL = 16 * 1024 * 1024
VMEM_SUBTRACT = 40 * 1024 * 1024


def body(images, coeffs, weights, scales, valid_epoch, patch_owner, patch_local):
    band_count = lax.axis_size("band")
    _, epochs, per_epoch, tile_rows, _ = images.shape
    up = gather_stages(band_count)
    me = lax.axis_index("band").astype(jnp.int32).reshape(1)
    owners = patch_owner.reshape(epochs, per_epoch)
    locals_ = patch_local.reshape(epochs, per_epoch)

    smoothed, *messages = smooth(
        me, coeffs[0].transpose(2, 0, 1), weights, valid_epoch, owners, locals_, images[0], up, band_count)

    def exchange(value, step):
        return lax.ppermute(value, "band", [(d, d ^ step) for d in range(band_count)])

    first, second, third = up
    half = third // 2
    stride = first * second
    groups = send_groups(third)
    arrived = []
    for g, (low, high) in enumerate(groups):
        parts = [messages[g]] + [
            exchange(messages[j * len(groups) + g], j) for j in range(1, first)]
        split = add_and_split(parts, second, minor=True)
        parts = [split[0]] + [exchange(split[j], j * first) for j in range(1, second)]
        split = add_and_split(parts, high - low)
        for digit in reversed(range(low, high)):
            block = split[digit - low]
            arrived.append(exchange(block, digit * stride) if digit else block)

    pieces = [finish(arrived, tile_rows)]
    own = pieces[0]
    distant = [exchange(own, j * stride) for j in reversed(range(half, third))][::-1]
    close = [own] + [exchange(own, j * stride) for j in range(1, half)]
    halves = [join(close) if len(close) > 1 else close[0], join(distant) if len(distant) > 1 else distant[0]]
    pieces = []
    for piece in halves:
        pieces.append([piece] + [exchange(piece, j * first) for j in range(1, second)])
    pieces = [piece for pair in zip(*pieces) for piece in pair]
    pieces = pieces + [exchange(piece, j) for j in range(1, first) for piece in pieces]

    difference, templates = subtract(me, scales, owners, locals_, pieces, smoothed, up)
    return difference[None], templates


def solution(mesh):
    return jax.shard_map(
        body,
        mesh=mesh,
        in_specs=(
            P(("groups", "band"), None, None, None, None),
            P(("groups", "band"), None, None, None),
            P(("groups", "band"), None),
            P(("groups", "band"), None),
            P(("groups", "band"), None),
            P(("groups", "band"), None, None, None),
            P(("groups", "band"), None, None),
        ),
        out_specs=(
            P(("groups", "band"), None, None, None, None),
            P(("groups", "band"), None, None),
        ),
        check_vma=False,
    )
```

```python
import functools

import jax
import jax.numpy as jnp
import numpy as np
from jax import lax
from jax.experimental import pallas as pl
from jax.experimental.pallas import tpu as pltpu
from jax.sharding import PartitionSpec as P


PD = 4
HALF = 9
P_SIZE = 3

sigmas = (0.75, 1.5, 3.0)
degrees = (4, 2, 2)

BF16 = jnp.bfloat16
F32 = jnp.float32
EXTRA = 8


def kernel_matrices(tile_side):
    place = np.arange(tile_side)
    apart = place[:, None] - place[None, :]
    offset = apart.astype(np.float32)
    inside = (np.abs(apart) <= HALF).astype(np.float32)
    taps = np.arange(-HALF, HALF + 1).astype(np.float32)
    tables = []
    for width_sigma, degree in zip(sigmas, degrees):
        scale = np.float32(2.0 * width_sigma * width_sigma)
        total = np.sum(np.exp(-taps * taps / scale), dtype=np.float32)
        envelope = np.exp(-offset * offset / scale) * inside / total
        for power in range(degree + 1):
            tables.append((envelope * (offset / np.float32(width_sigma)) ** power).astype(np.float32))
    return np.stack(tables)


def basis_pairs():
    kernel_list = []
    base_index = 0
    for degree in degrees:
        for column_power in range(degree + 1):
            for row_power in range(degree + 1 - column_power):
                kernel_list.append((base_index + row_power, base_index + column_power))
        base_index = base_index + degree + 1
    return kernel_list


def gather_stages(band_count):
    rest = band_count // 2
    inner = 1
    while 4 * inner * inner <= rest:
        inner *= 2
    return [factor for factor in (2, inner, rest // inner) if factor > 1]


def place_of(distance, factors):
    total = int(np.prod(factors))
    place = 0
    for factor in factors:
        total //= factor
        place = place + (distance & (factor - 1)) * total
        distance = distance >> (factor.bit_length() - 1)
    return place


def send_groups(third):
    half = third // 2
    if third > 4:
        return [(half, third), (0, half)]
    return [(digit, digit + 1) for digit in reversed(range(half, third))] + [(0, half)]


def send_place(distance, stages):
    first, second, third = stages
    over = distance >> (first.bit_length() - 1)
    along = over >> (second.bit_length() - 1)
    return ((distance & (first - 1)) * third + along) * second + (over & (second - 1))


def smooth_kernel(
    me_ref, weight_hbm, valid_hbm, owner_hbm, local_hbm, coef_hbm, spread_hbm, column_hbm, row_hbm, image_hbm,
    smooth_ref, *rest, factors, row_count, layers,
):
    first, second, third = factors
    starts = [(core * third + low) * second for core in range(first) for low, high in send_groups(third)]
    message_refs, rest = rest[:len(starts)], rest[len(starts):]
    weight_ref, valid_ref, owner_ref, local_ref, coef_ref, spread_ref, column_ref, row_ref, held_ref = rest[:9]
    small_sems, image_sems, total_ref, factor_ref = rest[9:13]
    mixer_refs, column_pass_refs = rest[13:13 + 2 * TOGETHER], rest[13 + 2 * TOGETHER:]
    epochs, per_epoch, tile_rows, tile_side = smooth_ref.shape
    depth = row_count * tile_rows

    small = [pltpu.make_async_copy(source, target, small_sems.at[k]) for k, (source, target) in enumerate((
        (coef_hbm, coef_ref), (spread_hbm, spread_ref), (row_hbm, row_ref), (column_hbm, column_ref),
        (weight_hbm, weight_ref), (valid_hbm, valid_ref), (owner_hbm, owner_ref), (local_hbm, local_ref)))]
    images = [
        pltpu.make_async_copy(image_hbm.at[epoch], held_ref.at[epoch], image_sems.at[epoch])
        for epoch in range(epochs)]
    for copy in small[:4] + images[:TOGETHER] + small[4:] + images[TOGETHER:]:
        copy.start()

    total_ref[...] = jnp.zeros_like(total_ref)
    small[0].wait()
    small[1].wait()
    left = coef_ref[...].reshape(P_SIZE * epochs, coef_ref.shape[2])
    spread_coefs = None
    for _ in range(3):
        piece = left.astype(BF16)
        left = left - piece.astype(F32)
        term = jnp.dot(piece, spread_ref[...], preferred_element_type=F32)
        spread_coefs = term if spread_coefs is None else spread_coefs + term
    for k in range(len(layers)):
        factor_ref[k] = spread_coefs[:, k * tile_side:(k + 1) * tile_side]
    for copy in small[2:]:
        copy.wait()

    row = lax.broadcasted_iota(jnp.int32, (tile_rows, tile_side), 0).astype(F32)
    lane = lax.broadcasted_iota(jnp.int32, (8, tile_side), 1)
    column = lane.astype(F32)
    down = 2.0 * (row + 0.5) / tile_rows - 1.0

    def mixers(epoch, mixer_ref):
        for block in range(mixer_ref.shape[0]):
            sums = []
            for m in range(P_SIZE):
                value = None
                for k, owner in enumerate(layers):
                    if owner == block:
                        factor = factor_ref[k, m * epochs + epoch:m * epochs + epoch + 1, :]
                        term = factor * row_ref[k]
                        value = term if value is None else value + term
                sums.append(value)
            mixer_ref[block, :tile_rows] = (sums[0] + down * sums[2]).astype(BF16)
            mixer_ref[block, tile_rows:] = sums[1].astype(BF16)

    def column_pass(epoch, column_pass_ref):
        pixels = held_ref[epoch].reshape(per_epoch * tile_rows, tile_side).astype(BF16)
        for c in range(0, row_count, 2):
            wide = min(2, row_count - c)
            passed = jnp.dot(
                pixels, column_ref[:, c * tile_side:(c + wide) * tile_side], preferred_element_type=F32).astype(BF16)
            for s in range(wide):
                for t in range(per_epoch):
                    column_pass_ref[t, (c + s) * tile_rows:(c + s + 1) * tile_rows] = (
                        passed[t * tile_rows:(t + 1) * tile_rows, s * tile_side:(s + 1) * tile_side])

    def row_pass(epoch, mixer_ref, column_pass_ref):
        mixer = jnp.concatenate([mixer_ref[block] for block in range(mixer_ref.shape[0])], axis=1)[:, :depth]
        weight = jnp.full((8, tile_side), weight_ref[0, epoch] * valid_ref[0, epoch].astype(F32), F32)
        weight = weight.astype(BF16).astype(F32)
        weights = jnp.concatenate([weight] * (tile_rows // 8), axis=0)
        for left in range(0, per_epoch, 2):
            both = jnp.concatenate([column_pass_ref[left], column_pass_ref[left + 1]], axis=1)
            spatial = jnp.dot(mixer, both, preferred_element_type=F32)
            for s in range(2):
                t = left + s
                across = (column + (t * tile_side + 0.5)) * (2.0 / (per_epoch * tile_side)) - 1.0
                across = jnp.concatenate([across] * (tile_rows // 8), axis=0)
                part = spatial[:, s * tile_side:(s + 1) * tile_side]
                value = part[:tile_rows] + across * part[tile_rows:]
                smooth_ref[epoch, t] = value
                place = send_place(owner_ref[epoch, t] ^ me_ref[0], factors) * PD + local_ref[epoch, t]
                total_ref[place, :tile_rows] = (
                    total_ref[place, :tile_rows] + weights * value)
                total_ref[place, tile_rows:] = (
                    total_ref[place, tile_rows:] + jnp.where(lane == t % tile_side, weight, 0.0))

    for step in range(epochs // TOGETHER + 1):
        now = range(step * TOGETHER, min(epochs, (step + 1) * TOGETHER))
        for epoch in now:
            images[epoch].wait()
        before = range((step - 1) * TOGETHER, step * TOGETHER) if step else ()
        for k in range(TOGETHER):
            for epoch in now[k:k + 1]:
                column_pass(epoch, column_pass_refs[epoch % (2 * TOGETHER)])
                mixers(epoch, mixer_refs[epoch % (2 * TOGETHER)])
            for epoch in before[k:k + 1]:
                slot = epoch % (2 * TOGETHER)
                row_pass(epoch, mixer_refs[slot], column_pass_refs[slot])

    line = lax.broadcasted_iota(jnp.int32, (8, tile_side), 0)
    for start, message_ref in zip(starts, message_refs):
        @pl.loop(0, message_ref.shape[0])
        def _(i):
            block = (start + i) * PD
            marks = jnp.zeros((8, tile_side), F32)
            for q in range(PD):
                message_ref[i, q * tile_rows:(q + 1) * tile_rows, :] = (
                    total_ref[block + q, :tile_rows].astype(BF16))
                marks = jnp.where(line == q, total_ref[block + q, tile_rows:], marks)
            message_ref[i, PD * tile_rows:, :] = marks.astype(BF16)


VMEM = pl.BlockSpec(memory_space=pltpu.VMEM)
SMEM = pl.BlockSpec(memory_space=pltpu.SMEM)


def smooth(me, coeffs, weights, valid_epoch, owners, locals_, images, factors, band_count):
    epochs, per_epoch, tile_rows, tile_side = images.shape
    columns = kernel_matrices(tile_side)
    row_count = columns.shape[0]
    columns = jnp.asarray(columns.transpose(2, 0, 1).reshape(tile_side, row_count * tile_side), BF16)
    per_lanes = tile_side // tile_rows
    row_matrices = np.asarray(kernel_matrices(tile_rows), dtype=BF16).astype(np.float32)
    pairs = basis_pairs()
    layers, rows, spread = [], [], []
    for block in range(-(-row_count // per_lanes)):
        held = [[b for b, pair in enumerate(pairs) if pair[1] == block * per_lanes + i] for i in range(per_lanes)]
        for depth in range(max(map(len, held))):
            layers.append(block)
            rows.append(np.zeros((tile_rows, tile_side), np.float32))
            spread.append(np.zeros((len(pairs), tile_side), np.float32))
            for i, bases in enumerate(held):
                if depth < len(bases):
                    lanes = slice(i * tile_rows, (i + 1) * tile_rows)
                    rows[-1][:, lanes] = row_matrices[pairs[bases[depth]][0]]
                    spread[-1][bases[depth], lanes] = 1.0
    rows = jnp.asarray(np.stack(rows))
    spread = jnp.asarray(np.concatenate(spread, axis=1), BF16)
    block_rows = PD * tile_rows + EXTRA
    first, second, third = factors
    messages = [
        jax.ShapeDtypeStruct(((high - low) * second, block_rows, tile_side), BF16)
        for _ in range(first) for low, high in send_groups(third)]
    return pl.pallas_call(
        functools.partial(smooth_kernel, factors=factors, row_count=row_count,
            layers=layers),
        in_specs=[SMEM] + [pl.BlockSpec(memory_space=pltpu.HBM)] * 9,
        out_specs=[VMEM] * (1 + len(messages)),
        out_shape=[jax.ShapeDtypeStruct(images.shape, F32)] + messages,
        scratch_shapes=[
            *(pltpu.SMEM(value.shape, value.dtype) for value in (weights, valid_epoch, owners, locals_)),
            *(pltpu.VMEM(value.shape, value.dtype) for value in (coeffs, spread, columns, rows, images)),
            pltpu.SemaphoreType.DMA((8,)),
            pltpu.SemaphoreType.DMA((epochs,)),
            pltpu.VMEM((band_count * PD, tile_rows + 8, tile_side), F32),
            pltpu.VMEM((len(layers), P_SIZE * epochs, tile_side), F32),
        ] + [
            pltpu.VMEM((-(-row_count // per_lanes), 2 * tile_rows, tile_side), BF16),
        ] * (2 * TOGETHER) + [
            pltpu.VMEM((per_epoch, row_count * tile_rows, tile_side), BF16),
        ] * (2 * TOGETHER),
        compiler_params=pltpu.CompilerParams(vmem_limit_bytes=VMEM_SMOOTH),
        name="smooth",
    )(me, *[pltpu.with_memory_space_constraint(value, pltpu.HBM) for value in (
        weights, valid_epoch, owners, locals_, coeffs, spread, columns, rows, images)])


def add_kernel(*refs, count, groups, minor):
    parts, outs = refs[:count], refs[count:]
    per_group = outs[0].shape[0]
    for g in range(groups):
        for i in range(per_group):
            place = i * groups + g if minor else g * per_group + i
            total = parts[0][place].astype(F32)
            for part in parts[1:]:
                total = total + part[place].astype(F32)
            outs[g][i] = total.astype(BF16)


def add_and_split(parts, groups, minor=False):
    blocks, block_rows, lanes = parts[0].shape
    out = jax.ShapeDtypeStruct((blocks // groups, block_rows, lanes), BF16)
    return pl.pallas_call(
        functools.partial(add_kernel, count=len(parts), groups=groups, minor=minor),
        in_specs=[VMEM] * len(parts), out_specs=[VMEM] * groups,
        out_shape=[out] * groups, name="add_and_split",
        compiler_params=pltpu.CompilerParams(vmem_limit_bytes=VMEM_SMALL),
    )(*parts)


def finish_kernel(*refs):
    *parts, out_ref = refs
    tile_rows = out_ref.shape[1]
    total = parts[0][0].astype(F32)
    for part in parts[1:]:
        total = total + part[0].astype(F32)
    marks = total[PD * tile_rows:, :]
    inverse = jnp.broadcast_to(1.0 / (1.0 + jnp.sum(marks, axis=1, keepdims=True)), marks.shape)
    for q in range(PD):
        out_ref[q] = (total[q * tile_rows:(q + 1) * tile_rows] * inverse[q:q + 1]).astype(BF16)


def finish(parts, tile_rows):
    return pl.pallas_call(
        finish_kernel, in_specs=[VMEM] * len(parts), out_specs=VMEM,
        out_shape=jax.ShapeDtypeStruct((PD, tile_rows, parts[0].shape[2]), BF16), name="finish",
        compiler_params=pltpu.CompilerParams(vmem_limit_bytes=VMEM_SMALL),
    )(*parts)


def join_kernel(*refs):
    start = 0
    for piece in refs[:-1]:
        refs[-1][start:start + piece.shape[0]] = piece[...]
        start += piece.shape[0]


def join(pieces):
    total = sum(piece.shape[0] for piece in pieces)
    return pl.pallas_call(
        join_kernel, in_specs=[VMEM] * len(pieces), out_specs=VMEM,
        out_shape=jax.ShapeDtypeStruct((total, *pieces[0].shape[1:]), BF16), name="join",
        compiler_params=pltpu.CompilerParams(vmem_limit_bytes=VMEM_SMALL),
    )(*pieces)


def difference_kernel(me_ref, scale_ref, owner_ref, local_ref, smooth_ref, *rest, factors, count):
    pieces, (out_ref, template_ref, table_ref, ready_ref, sems) = rest[:count], rest[count:]
    epochs, per_epoch = smooth_ref.shape[:2]
    start = 0
    for piece in pieces:
        table_ref[start:start + piece.shape[0]] = piece[...]
        start += piece.shape[0]

    def copy(e):
        return pltpu.make_async_copy(ready_ref.at[e], out_ref.at[e], sems.at[e])

    for e in range(epochs):
        scale = scale_ref[0, e]
        for t in range(per_epoch):
            place = place_of(owner_ref[e, t] ^ me_ref[0], factors) * PD + local_ref[e, t]
            ready_ref[e, t] = smooth_ref[e, t] - scale * table_ref[place].astype(F32)
        if e > 0:
            copy(e - 1).start()
    template_ref[...] = table_ref[:PD]
    copy(epochs - 1).start()
    for e in range(epochs):
        copy(e).wait()


def subtract(me, scales, owners, locals_, pieces, smoothed, factors):
    tile_rows, tile_side = smoothed.shape[2:]
    own = (PD, tile_rows, tile_side)
    return pl.pallas_call(
        functools.partial(difference_kernel, factors=factors, count=len(pieces)),
        in_specs=[SMEM] * 4 + [VMEM] * (1 + len(pieces)),
        out_specs=[pl.BlockSpec(memory_space=pltpu.HBM), VMEM],
        out_shape=[jax.ShapeDtypeStruct(smoothed.shape, F32), jax.ShapeDtypeStruct(own, BF16)],
        scratch_shapes=[
            pltpu.VMEM((PD * int(np.prod(factors)), tile_rows, tile_side), BF16),
            pltpu.VMEM(smoothed.shape, F32),
            pltpu.SemaphoreType.DMA((smoothed.shape[0],)),
        ],
        compiler_params=pltpu.CompilerParams(vmem_limit_bytes=VMEM_SUBTRACT),
        name="subtract",
    )(me, scales, owners, locals_, smoothed, *pieces)


TOGETHER = 4
VMEM_SMOOTH = 48 * 1024 * 1024
VMEM_SMALL = 16 * 1024 * 1024
VMEM_SUBTRACT = 40 * 1024 * 1024


def body(images, coeffs, weights, scales, valid_epoch, patch_owner, patch_local):
    band_count = lax.axis_size("band")
    _, epochs, per_epoch, tile_rows, _ = images.shape
    up = gather_stages(band_count)
    me = lax.axis_index("band").astype(jnp.int32).reshape(1)
    owners = patch_owner.reshape(epochs, per_epoch)
    locals_ = patch_local.reshape(epochs, per_epoch)

    smoothed, *messages = smooth(
        me, coeffs[0].transpose(2, 0, 1), weights, valid_epoch, owners, locals_, images[0], up, band_count)

    def exchange(value, step):
        return lax.ppermute(value, "band", [(d, d ^ step) for d in range(band_count)])

    first, second, third = up
    half = third // 2
    stride = first * second
    groups = send_groups(third)
    arrived = []
    for g, (low, high) in enumerate(groups):
        parts = [messages[g]] + [
            exchange(messages[j * len(groups) + g], j) for j in range(1, first)]
        split = add_and_split(parts, second, minor=True)
        parts = [split[0]] + [exchange(split[j], j * first) for j in range(1, second)]
        split = add_and_split(parts, high - low)
        for digit in reversed(range(low, high)):
            block = split[digit - low]
            arrived.append(exchange(block, digit * stride) if digit else block)

    pieces = [finish(arrived, tile_rows)]
    own = pieces[0]
    distant = [exchange(own, j * stride) for j in reversed(range(half, third))][::-1]
    close = [own] + [exchange(own, j * stride) for j in range(1, half)]
    halves = [join(close) if len(close) > 1 else close[0], join(distant) if len(distant) > 1 else distant[0]]
    pieces = []
    for piece in halves:
        pieces.append([piece] + [exchange(piece, j * first) for j in range(1, second)])
    pieces = [piece for pair in zip(*pieces) for piece in pair]
    pieces = pieces + [exchange(piece, j) for j in range(1, first) for piece in pieces]

    difference, templates = subtract(me, scales, owners, locals_, pieces, smoothed, up)
    return difference[None], templates


def solution(mesh):
    return jax.shard_map(
        body,
        mesh=mesh,
        in_specs=(
            P(("groups", "band"), None, None, None, None),
            P(("groups", "band"), None, None, None),
            P(("groups", "band"), None),
            P(("groups", "band"), None),
            P(("groups", "band"), None),
            P(("groups", "band"), None, None, None),
            P(("groups", "band"), None, None),
        ),
        out_specs=(
            P(("groups", "band"), None, None, None, None),
            P(("groups", "band"), None, None),
        ),
        check_vma=False,
    )
```

```python
import functools

import jax
import jax.numpy as jnp
import numpy as np
from jax import lax
from jax.experimental import pallas as pl
from jax.experimental.pallas import tpu as pltpu
from jax.sharding import PartitionSpec as P


PD = 4
HALF = 9
P_SIZE = 3

sigmas = (0.75, 1.5, 3.0)
degrees = (4, 2, 2)

BF16 = jnp.bfloat16
F32 = jnp.float32
EXTRA = 8


def kernel_matrices(tile_side):
    place = np.arange(tile_side)
    apart = place[:, None] - place[None, :]
    offset = apart.astype(np.float32)
    inside = (np.abs(apart) <= HALF).astype(np.float32)
    taps = np.arange(-HALF, HALF + 1).astype(np.float32)
    tables = []
    for width_sigma, degree in zip(sigmas, degrees):
        scale = np.float32(2.0 * width_sigma * width_sigma)
        total = np.sum(np.exp(-taps * taps / scale), dtype=np.float32)
        envelope = np.exp(-offset * offset / scale) * inside / total
        for power in range(degree + 1):
            tables.append((envelope * (offset / np.float32(width_sigma)) ** power).astype(np.float32))
    return np.stack(tables)


def basis_pairs():
    kernel_list = []
    base_index = 0
    for degree in degrees:
        for column_power in range(degree + 1):
            for row_power in range(degree + 1 - column_power):
                kernel_list.append((base_index + row_power, base_index + column_power))
        base_index = base_index + degree + 1
    return kernel_list


def gather_stages(band_count):
    rest = band_count // 2
    inner = 1
    while 4 * inner * inner <= rest:
        inner *= 2
    return [factor for factor in (2, inner, rest // inner) if factor > 1]


def place_of(distance, factors):
    total = int(np.prod(factors))
    place = 0
    for factor in factors:
        total //= factor
        place = place + (distance & (factor - 1)) * total
        distance = distance >> (factor.bit_length() - 1)
    return place


def send_groups(third):
    half = third // 2
    if third > 4:
        return [(half, third), (0, half)]
    return [(digit, digit + 1) for digit in reversed(range(half, third))] + [(0, half)]


def send_place(distance, stages):
    first, second, third = stages
    over = distance >> (first.bit_length() - 1)
    along = over >> (second.bit_length() - 1)
    return ((distance & (first - 1)) * third + along) * second + (over & (second - 1))


def smooth_kernel(
    me_ref, weight_hbm, valid_hbm, owner_hbm, local_hbm, coef_hbm, spread_hbm, column_hbm, row_hbm, image_hbm,
    smooth_ref, *rest, factors, row_count, layers,
):
    first, second, third = factors
    starts = [(core * third + low) * second for core in range(first) for low, high in send_groups(third)]
    message_refs, rest = rest[:len(starts)], rest[len(starts):]
    weight_ref, valid_ref, owner_ref, local_ref, coef_ref, spread_ref, column_ref, row_ref, held_ref = rest[:9]
    small_sems, image_sems, total_ref, factor_ref = rest[9:13]
    mixer_refs, column_pass_refs = rest[13:13 + 2 * TOGETHER], rest[13 + 2 * TOGETHER:]
    epochs, per_epoch, tile_rows, tile_side = smooth_ref.shape
    depth = row_count * tile_rows

    small = [pltpu.make_async_copy(source, target, small_sems.at[k]) for k, (source, target) in enumerate((
        (coef_hbm, coef_ref), (spread_hbm, spread_ref), (row_hbm, row_ref), (column_hbm, column_ref),
        (weight_hbm, weight_ref), (valid_hbm, valid_ref), (owner_hbm, owner_ref), (local_hbm, local_ref)))]
    images = [
        pltpu.make_async_copy(image_hbm.at[epoch], held_ref.at[epoch], image_sems.at[epoch])
        for epoch in range(epochs)]
    for copy in small[:4] + images[:TOGETHER] + small[4:] + images[TOGETHER:]:
        copy.start()

    total_ref[...] = jnp.zeros_like(total_ref)
    small[0].wait()
    small[1].wait()
    left = coef_ref[...].reshape(P_SIZE * epochs, coef_ref.shape[2])
    spread_coefs = None
    for _ in range(3):
        piece = left.astype(BF16)
        left = left - piece.astype(F32)
        term = jnp.dot(piece, spread_ref[...], preferred_element_type=F32)
        spread_coefs = term if spread_coefs is None else spread_coefs + term
    for k in range(len(layers)):
        factor_ref[k] = spread_coefs[:, k * tile_side:(k + 1) * tile_side]
    for copy in small[2:]:
        copy.wait()

    row = lax.broadcasted_iota(jnp.int32, (tile_rows, tile_side), 0).astype(F32)
    lane = lax.broadcasted_iota(jnp.int32, (8, tile_side), 1)
    column = lane.astype(F32)
    down = 2.0 * (row + 0.5) / tile_rows - 1.0

    def mixers(epoch, mixer_ref):
        for block in range(mixer_ref.shape[0]):
            sums = []
            for m in range(P_SIZE):
                value = None
                for k, owner in enumerate(layers):
                    if owner == block:
                        factor = factor_ref[k, m * epochs + epoch:m * epochs + epoch + 1, :]
                        term = factor * row_ref[k]
                        value = term if value is None else value + term
                sums.append(value)
            mixer_ref[block, :tile_rows] = (sums[0] + down * sums[2]).astype(BF16)
            mixer_ref[block, tile_rows:] = sums[1].astype(BF16)

    def column_pass(epoch, column_pass_ref):
        pixels = held_ref[epoch].reshape(per_epoch * tile_rows, tile_side).astype(BF16)
        for c in range(0, row_count, 2):
            wide = min(2, row_count - c)
            passed = jnp.dot(
                pixels, column_ref[:, c * tile_side:(c + wide) * tile_side], preferred_element_type=F32).astype(BF16)
            for s in range(wide):
                for t in range(per_epoch):
                    column_pass_ref[t, (c + s) * tile_rows:(c + s + 1) * tile_rows] = (
                        passed[t * tile_rows:(t + 1) * tile_rows, s * tile_side:(s + 1) * tile_side])

    def row_pass(epoch, mixer_ref, column_pass_ref):
        mixer = jnp.concatenate([mixer_ref[block] for block in range(mixer_ref.shape[0])], axis=1)[:, :depth]
        weight = jnp.full((8, tile_side), weight_ref[0, epoch] * valid_ref[0, epoch].astype(F32), F32)
        weight = weight.astype(BF16).astype(F32)
        weights = jnp.concatenate([weight] * (tile_rows // 8), axis=0)
        for left in range(0, per_epoch, 2):
            both = jnp.concatenate([column_pass_ref[left], column_pass_ref[left + 1]], axis=1)
            spatial = jnp.dot(mixer, both, preferred_element_type=F32)
            for s in range(2):
                t = left + s
                across = (column + (t * tile_side + 0.5)) * (2.0 / (per_epoch * tile_side)) - 1.0
                across = jnp.concatenate([across] * (tile_rows // 8), axis=0)
                part = spatial[:, s * tile_side:(s + 1) * tile_side]
                value = part[:tile_rows] + across * part[tile_rows:]
                smooth_ref[epoch, t] = value
                place = send_place(owner_ref[epoch, t] ^ me_ref[0], factors) * PD + local_ref[epoch, t]
                total_ref[place, :tile_rows] = (
                    total_ref[place, :tile_rows] + weights * value)
                total_ref[place, tile_rows:] = (
                    total_ref[place, tile_rows:] + jnp.where(lane == t % tile_side, weight, 0.0))

    for step in range(epochs // TOGETHER + 1):
        now = range(step * TOGETHER, min(epochs, (step + 1) * TOGETHER))
        for epoch in now:
            images[epoch].wait()
        before = range((step - 1) * TOGETHER, step * TOGETHER) if step else ()
        for k in range(TOGETHER):
            for epoch in now[k:k + 1]:
                column_pass(epoch, column_pass_refs[epoch % (2 * TOGETHER)])
                mixers(epoch, mixer_refs[epoch % (2 * TOGETHER)])
            for epoch in before[k:k + 1]:
                slot = epoch % (2 * TOGETHER)
                row_pass(epoch, mixer_refs[slot], column_pass_refs[slot])

    line = lax.broadcasted_iota(jnp.int32, (8, tile_side), 0)
    for start, message_ref in zip(starts, message_refs):
        @pl.loop(0, message_ref.shape[0])
        def _(i):
            block = (start + i) * PD
            marks = jnp.zeros((8, tile_side), F32)
            for q in range(PD):
                message_ref[i, q * tile_rows:(q + 1) * tile_rows, :] = (
                    total_ref[block + q, :tile_rows].astype(BF16))
                marks = jnp.where(line == q, total_ref[block + q, tile_rows:], marks)
            message_ref[i, PD * tile_rows:, :] = marks.astype(BF16)


VMEM = pl.BlockSpec(memory_space=pltpu.VMEM)
SMEM = pl.BlockSpec(memory_space=pltpu.SMEM)


def smooth(me, coeffs, weights, valid_epoch, owners, locals_, images, factors, band_count):
    epochs, per_epoch, tile_rows, tile_side = images.shape
    columns = kernel_matrices(tile_side)
    row_count = columns.shape[0]
    columns = jnp.asarray(columns.transpose(2, 0, 1).reshape(tile_side, row_count * tile_side), BF16)
    per_lanes = tile_side // tile_rows
    row_matrices = np.asarray(kernel_matrices(tile_rows), dtype=BF16).astype(np.float32)
    pairs = basis_pairs()
    layers, rows, spread = [], [], []
    for block in range(-(-row_count // per_lanes)):
        held = [[b for b, pair in enumerate(pairs) if pair[1] == block * per_lanes + i] for i in range(per_lanes)]
        for depth in range(max(map(len, held))):
            layers.append(block)
            rows.append(np.zeros((tile_rows, tile_side), np.float32))
            spread.append(np.zeros((len(pairs), tile_side), np.float32))
            for i, bases in enumerate(held):
                if depth < len(bases):
                    lanes = slice(i * tile_rows, (i + 1) * tile_rows)
                    rows[-1][:, lanes] = row_matrices[pairs[bases[depth]][0]]
                    spread[-1][bases[depth], lanes] = 1.0
    rows = jnp.asarray(np.stack(rows))
    spread = jnp.asarray(np.concatenate(spread, axis=1), BF16)
    block_rows = PD * tile_rows + EXTRA
    first, second, third = factors
    messages = [
        jax.ShapeDtypeStruct(((high - low) * second, block_rows, tile_side), BF16)
        for _ in range(first) for low, high in send_groups(third)]
    return pl.pallas_call(
        functools.partial(smooth_kernel, factors=factors, row_count=row_count,
            layers=layers),
        in_specs=[SMEM] + [pl.BlockSpec(memory_space=pltpu.HBM)] * 9,
        out_specs=[VMEM] * (1 + len(messages)),
        out_shape=[jax.ShapeDtypeStruct(images.shape, F32)] + messages,
        scratch_shapes=[
            *(pltpu.SMEM(value.shape, value.dtype) for value in (weights, valid_epoch, owners, locals_)),
            *(pltpu.VMEM(value.shape, value.dtype) for value in (coeffs, spread, columns, rows, images)),
            pltpu.SemaphoreType.DMA((8,)),
            pltpu.SemaphoreType.DMA((epochs,)),
            pltpu.VMEM((band_count * PD, tile_rows + 8, tile_side), F32),
            pltpu.VMEM((len(layers), P_SIZE * epochs, tile_side), F32),
        ] + [
            pltpu.VMEM((-(-row_count // per_lanes), 2 * tile_rows, tile_side), BF16),
        ] * (2 * TOGETHER) + [
            pltpu.VMEM((per_epoch, row_count * tile_rows, tile_side), BF16),
        ] * (2 * TOGETHER),
        compiler_params=pltpu.CompilerParams(vmem_limit_bytes=VMEM_SMOOTH),
        name="smooth",
    )(me, *[pltpu.with_memory_space_constraint(value, pltpu.HBM) for value in (
        weights, valid_epoch, owners, locals_, coeffs, spread, columns, rows, images)])


def add_kernel(*refs, count, groups, minor):
    parts, outs = refs[:count], refs[count:]
    per_group = outs[0].shape[0]
    for g in range(groups):
        for i in range(per_group):
            place = i * groups + g if minor else g * per_group + i
            total = parts[0][place].astype(F32)
            for part in parts[1:]:
                total = total + part[place].astype(F32)
            outs[g][i] = total.astype(BF16)


def add_and_split(parts, groups, minor=False):
    blocks, block_rows, lanes = parts[0].shape
    out = jax.ShapeDtypeStruct((blocks // groups, block_rows, lanes), BF16)
    return pl.pallas_call(
        functools.partial(add_kernel, count=len(parts), groups=groups, minor=minor),
        in_specs=[VMEM] * len(parts), out_specs=[VMEM] * groups,
        out_shape=[out] * groups, name="add_and_split",
        compiler_params=pltpu.CompilerParams(vmem_limit_bytes=VMEM_SMALL),
    )(*parts)


def finish_kernel(*refs):
    *parts, out_ref = refs
    tile_rows = out_ref.shape[1]
    total = parts[0][0].astype(F32)
    for part in parts[1:]:
        total = total + part[0].astype(F32)
    marks = total[PD * tile_rows:, :]
    inverse = jnp.broadcast_to(1.0 / (1.0 + jnp.sum(marks, axis=1, keepdims=True)), marks.shape)
    for q in range(PD):
        out_ref[q] = (total[q * tile_rows:(q + 1) * tile_rows] * inverse[q:q + 1]).astype(BF16)


def finish(parts, tile_rows):
    return pl.pallas_call(
        finish_kernel, in_specs=[VMEM] * len(parts), out_specs=VMEM,
        out_shape=jax.ShapeDtypeStruct((PD, tile_rows, parts[0].shape[2]), BF16), name="finish",
        compiler_params=pltpu.CompilerParams(vmem_limit_bytes=VMEM_SMALL),
    )(*parts)


def join_kernel(*refs):
    start = 0
    for piece in refs[:-1]:
        refs[-1][start:start + piece.shape[0]] = piece[...]
        start += piece.shape[0]


def join(pieces):
    total = sum(piece.shape[0] for piece in pieces)
    return pl.pallas_call(
        join_kernel, in_specs=[VMEM] * len(pieces), out_specs=VMEM,
        out_shape=jax.ShapeDtypeStruct((total, *pieces[0].shape[1:]), BF16), name="join",
        compiler_params=pltpu.CompilerParams(vmem_limit_bytes=VMEM_SMALL),
    )(*pieces)


def difference_kernel(me_ref, scale_ref, owner_ref, local_ref, smooth_ref, *rest, factors, count):
    pieces, (out_ref, template_ref, table_ref, ready_ref, sems) = rest[:count], rest[count:]
    epochs, per_epoch = smooth_ref.shape[:2]
    start = 0
    for piece in pieces:
        table_ref[start:start + piece.shape[0]] = piece[...]
        start += piece.shape[0]

    part = max(1, per_epoch // 2)
    parts = [(e, first) for e in range(epochs) for first in range(0, per_epoch, part)]

    def copy(k):
        e, first = parts[k]
        return pltpu.make_async_copy(
            ready_ref.at[e, first:first + part], out_ref.at[e, first:first + part], sems.at[k])

    for k, (e, first) in enumerate(parts):
        scale = scale_ref[0, e]
        for t in range(first, min(first + part, per_epoch)):
            place = place_of(owner_ref[e, t] ^ me_ref[0], factors) * PD + local_ref[e, t]
            ready_ref[e, t] = smooth_ref[e, t] - scale * table_ref[place].astype(F32)
        if k > 0:
            copy(k - 1).start()
    template_ref[...] = table_ref[:PD]
    copy(len(parts) - 1).start()
    for k in range(len(parts)):
        copy(k).wait()


def subtract(me, scales, owners, locals_, pieces, smoothed, factors):
    tile_rows, tile_side = smoothed.shape[2:]
    own = (PD, tile_rows, tile_side)
    return pl.pallas_call(
        functools.partial(difference_kernel, factors=factors, count=len(pieces)),
        in_specs=[SMEM] * 4 + [VMEM] * (1 + len(pieces)),
        out_specs=[pl.BlockSpec(memory_space=pltpu.HBM), VMEM],
        out_shape=[jax.ShapeDtypeStruct(smoothed.shape, F32), jax.ShapeDtypeStruct(own, BF16)],
        scratch_shapes=[
            pltpu.VMEM((PD * int(np.prod(factors)), tile_rows, tile_side), BF16),
            pltpu.VMEM(smoothed.shape, F32),
            pltpu.SemaphoreType.DMA((2 * smoothed.shape[0],)),
        ],
        compiler_params=pltpu.CompilerParams(vmem_limit_bytes=VMEM_SUBTRACT),
        name="subtract",
    )(me, scales, owners, locals_, smoothed, *pieces)


TOGETHER = 4
VMEM_SMOOTH = 48 * 1024 * 1024
VMEM_SMALL = 16 * 1024 * 1024
VMEM_SUBTRACT = 40 * 1024 * 1024


def body(images, coeffs, weights, scales, valid_epoch, patch_owner, patch_local):
    band_count = lax.axis_size("band")
    _, epochs, per_epoch, tile_rows, _ = images.shape
    up = gather_stages(band_count)
    me = lax.axis_index("band").astype(jnp.int32).reshape(1)
    owners = patch_owner.reshape(epochs, per_epoch)
    locals_ = patch_local.reshape(epochs, per_epoch)

    smoothed, *messages = smooth(
        me, coeffs[0].transpose(2, 0, 1), weights, valid_epoch, owners, locals_, images[0], up, band_count)

    def exchange(value, step):
        return lax.ppermute(value, "band", [(d, d ^ step) for d in range(band_count)])

    first, second, third = up
    half = third // 2
    stride = first * second
    groups = send_groups(third)
    arrived = []
    for g, (low, high) in enumerate(groups):
        parts = [messages[g]] + [
            exchange(messages[j * len(groups) + g], j) for j in range(1, first)]
        split = add_and_split(parts, second, minor=True)
        parts = [split[0]] + [exchange(split[j], j * first) for j in range(1, second)]
        split = add_and_split(parts, high - low)
        for digit in reversed(range(low, high)):
            block = split[digit - low]
            arrived.append(exchange(block, digit * stride) if digit else block)

    pieces = [finish(arrived, tile_rows)]
    own = pieces[0]
    distant = [exchange(own, j * stride) for j in reversed(range(half, third))][::-1]
    close = [own] + [exchange(own, j * stride) for j in range(1, half)]
    halves = [join(close) if len(close) > 1 else close[0], join(distant) if len(distant) > 1 else distant[0]]
    pieces = []
    for piece in halves:
        pieces.append([piece] + [exchange(piece, j * first) for j in range(1, second)])
    pieces = [piece for pair in zip(*pieces) for piece in pair]
    pieces = pieces + [exchange(piece, j) for j in range(1, first) for piece in pieces]

    difference, templates = subtract(me, scales, owners, locals_, pieces, smoothed, up)
    return difference[None], templates


def solution(mesh):
    return jax.shard_map(
        body,
        mesh=mesh,
        in_specs=(
            P(("groups", "band"), None, None, None, None),
            P(("groups", "band"), None, None, None),
            P(("groups", "band"), None),
            P(("groups", "band"), None),
            P(("groups", "band"), None),
            P(("groups", "band"), None, None, None),
            P(("groups", "band"), None, None),
        ),
        out_specs=(
            P(("groups", "band"), None, None, None, None),
            P(("groups", "band"), None, None),
        ),
        check_vma=False,
    )
```

```python
import functools

import jax
import jax.numpy as jnp
import numpy as np
from jax import lax
from jax.experimental import pallas as pl
from jax.experimental.pallas import tpu as pltpu
from jax.sharding import PartitionSpec as P


PD = 4
HALF = 9
P_SIZE = 3

sigmas = (0.75, 1.5, 3.0)
degrees = (4, 2, 2)

BF16 = jnp.bfloat16
F32 = jnp.float32
EXTRA = 8


def kernel_matrices(tile_side):
    place = np.arange(tile_side)
    apart = place[:, None] - place[None, :]
    offset = apart.astype(np.float32)
    inside = (np.abs(apart) <= HALF).astype(np.float32)
    taps = np.arange(-HALF, HALF + 1).astype(np.float32)
    tables = []
    for width_sigma, degree in zip(sigmas, degrees):
        scale = np.float32(2.0 * width_sigma * width_sigma)
        total = np.sum(np.exp(-taps * taps / scale), dtype=np.float32)
        envelope = np.exp(-offset * offset / scale) * inside / total
        for power in range(degree + 1):
            tables.append((envelope * (offset / np.float32(width_sigma)) ** power).astype(np.float32))
    return np.stack(tables)


def basis_pairs():
    kernel_list = []
    base_index = 0
    for degree in degrees:
        for column_power in range(degree + 1):
            for row_power in range(degree + 1 - column_power):
                kernel_list.append((base_index + row_power, base_index + column_power))
        base_index = base_index + degree + 1
    return kernel_list


def gather_stages(band_count):
    rest = band_count // 2
    inner = 1
    while 4 * inner * inner <= rest:
        inner *= 2
    return [factor for factor in (2, inner, rest // inner) if factor > 1]


def place_of(distance, factors):
    total = int(np.prod(factors))
    place = 0
    for factor in factors:
        total //= factor
        place = place + (distance & (factor - 1)) * total
        distance = distance >> (factor.bit_length() - 1)
    return place


def send_groups(third):
    half = third // 2
    if third > 4:
        return [(half, third), (0, half)]
    return [(digit, digit + 1) for digit in reversed(range(half, third))] + [(0, half)]


def send_place(distance, stages):
    first, second, third = stages
    over = distance >> (first.bit_length() - 1)
    along = over >> (second.bit_length() - 1)
    return ((distance & (first - 1)) * third + along) * second + (over & (second - 1))


def smooth_kernel(
    me_ref, weight_hbm, valid_hbm, owner_hbm, local_hbm, coef_hbm, spread_hbm, column_hbm, row_hbm, image_hbm,
    smooth_ref, *rest, factors, row_count, layers,
):
    first, second, third = factors
    starts = [(core * third + low) * second for core in range(first) for low, high in send_groups(third)]
    message_refs, rest = rest[:len(starts)], rest[len(starts):]
    weight_ref, valid_ref, owner_ref, local_ref, coef_ref, spread_ref, column_ref, row_ref, held_ref = rest[:9]
    small_sems, image_sems, total_ref, factor_ref = rest[9:13]
    mixer_refs, column_pass_refs = rest[13:13 + 2 * TOGETHER], rest[13 + 2 * TOGETHER:]
    epochs, per_epoch, tile_rows, tile_side = smooth_ref.shape
    depth = row_count * tile_rows

    small = [pltpu.make_async_copy(source, target, small_sems.at[k]) for k, (source, target) in enumerate((
        (coef_hbm, coef_ref), (spread_hbm, spread_ref), (row_hbm, row_ref), (column_hbm, column_ref),
        (weight_hbm, weight_ref), (valid_hbm, valid_ref), (owner_hbm, owner_ref), (local_hbm, local_ref)))]
    images = [
        pltpu.make_async_copy(image_hbm.at[epoch], held_ref.at[epoch], image_sems.at[epoch])
        for epoch in range(epochs)]
    for copy in small[:4] + images[:TOGETHER] + small[4:] + images[TOGETHER:]:
        copy.start()

    total_ref[...] = jnp.zeros_like(total_ref)
    small[0].wait()
    small[1].wait()
    left = coef_ref[...].reshape(P_SIZE * epochs, coef_ref.shape[2])
    spread_coefs = None
    for _ in range(3):
        piece = left.astype(BF16)
        left = left - piece.astype(F32)
        term = jnp.dot(piece, spread_ref[...], preferred_element_type=F32)
        spread_coefs = term if spread_coefs is None else spread_coefs + term
    for k in range(len(layers)):
        factor_ref[k] = spread_coefs[:, k * tile_side:(k + 1) * tile_side]
    for copy in small[2:]:
        copy.wait()

    row = lax.broadcasted_iota(jnp.int32, (tile_rows, tile_side), 0).astype(F32)
    lane = lax.broadcasted_iota(jnp.int32, (8, tile_side), 1)
    column = lane.astype(F32)
    down = 2.0 * (row + 0.5) / tile_rows - 1.0

    def mixers(epoch, mixer_ref):
        for block in range(mixer_ref.shape[0]):
            sums = []
            for m in range(P_SIZE):
                value = None
                for k, owner in enumerate(layers):
                    if owner == block:
                        factor = factor_ref[k, m * epochs + epoch:m * epochs + epoch + 1, :]
                        term = factor * row_ref[k]
                        value = term if value is None else value + term
                sums.append(value)
            mixer_ref[block, :tile_rows] = (sums[0] + down * sums[2]).astype(BF16)
            mixer_ref[block, tile_rows:] = sums[1].astype(BF16)

    def column_pass(epoch, column_pass_ref):
        pixels = held_ref[epoch].reshape(per_epoch * tile_rows, tile_side).astype(BF16)
        for c in range(0, row_count, 2):
            wide = min(2, row_count - c)
            passed = jnp.dot(
                pixels, column_ref[:, c * tile_side:(c + wide) * tile_side], preferred_element_type=F32).astype(BF16)
            for s in range(wide):
                for t in range(per_epoch):
                    column_pass_ref[t, (c + s) * tile_rows:(c + s + 1) * tile_rows] = (
                        passed[t * tile_rows:(t + 1) * tile_rows, s * tile_side:(s + 1) * tile_side])

    def row_pass(epoch, mixer_ref, column_pass_ref):
        mixer = jnp.concatenate([mixer_ref[block] for block in range(mixer_ref.shape[0])], axis=1)[:, :depth]
        weight = jnp.full((8, tile_side), weight_ref[0, epoch] * valid_ref[0, epoch].astype(F32), F32)
        weight = weight.astype(BF16).astype(F32)
        weights = jnp.concatenate([weight] * (tile_rows // 8), axis=0)
        for left in range(0, per_epoch, 2):
            both = jnp.concatenate([column_pass_ref[left], column_pass_ref[left + 1]], axis=1)
            spatial = jnp.dot(mixer, both, preferred_element_type=F32)
            for s in range(2):
                t = left + s
                across = (column + (t * tile_side + 0.5)) * (2.0 / (per_epoch * tile_side)) - 1.0
                across = jnp.concatenate([across] * (tile_rows // 8), axis=0)
                part = spatial[:, s * tile_side:(s + 1) * tile_side]
                value = part[:tile_rows] + across * part[tile_rows:]
                smooth_ref[epoch, t] = value
                place = send_place(owner_ref[epoch, t] ^ me_ref[0], factors) * PD + local_ref[epoch, t]
                total_ref[place, :tile_rows] = (
                    total_ref[place, :tile_rows] + weights * value)
                total_ref[place, tile_rows:] = (
                    total_ref[place, tile_rows:] + jnp.where(lane == t % tile_side, weight, 0.0))

    cuts = [0, *range(1, epochs, TOGETHER), epochs]
    steps = [range(a, b) for a, b in zip(cuts, cuts[1:])]
    for now, before in zip(steps + [range(0)], [range(0)] + steps):
        for epoch in now:
            images[epoch].wait()
        for k in range(TOGETHER):
            for epoch in now[k:k + 1]:
                slot = epoch % (2 * TOGETHER)
                column_pass(epoch, column_pass_refs[slot])
                mixers(epoch, mixer_refs[slot])
            for epoch in before[k:k + 1]:
                slot = epoch % (2 * TOGETHER)
                row_pass(epoch, mixer_refs[slot], column_pass_refs[slot])

    line = lax.broadcasted_iota(jnp.int32, (8, tile_side), 0)
    for start, message_ref in zip(starts, message_refs):
        @pl.loop(0, message_ref.shape[0])
        def _(i):
            block = (start + i) * PD
            marks = jnp.zeros((8, tile_side), F32)
            for q in range(PD):
                message_ref[i, q * tile_rows:(q + 1) * tile_rows, :] = (
                    total_ref[block + q, :tile_rows].astype(BF16))
                marks = jnp.where(line == q, total_ref[block + q, tile_rows:], marks)
            message_ref[i, PD * tile_rows:, :] = marks.astype(BF16)


VMEM = pl.BlockSpec(memory_space=pltpu.VMEM)
SMEM = pl.BlockSpec(memory_space=pltpu.SMEM)


def smooth(me, coeffs, weights, valid_epoch, owners, locals_, images, factors, band_count):
    epochs, per_epoch, tile_rows, tile_side = images.shape
    columns = kernel_matrices(tile_side)
    row_count = columns.shape[0]
    columns = jnp.asarray(columns.transpose(2, 0, 1).reshape(tile_side, row_count * tile_side), BF16)
    per_lanes = tile_side // tile_rows
    row_matrices = np.asarray(kernel_matrices(tile_rows), dtype=BF16).astype(np.float32)
    pairs = basis_pairs()
    layers, rows, spread = [], [], []
    for block in range(-(-row_count // per_lanes)):
        held = [[b for b, pair in enumerate(pairs) if pair[1] == block * per_lanes + i] for i in range(per_lanes)]
        for depth in range(max(map(len, held))):
            layers.append(block)
            rows.append(np.zeros((tile_rows, tile_side), np.float32))
            spread.append(np.zeros((len(pairs), tile_side), np.float32))
            for i, bases in enumerate(held):
                if depth < len(bases):
                    lanes = slice(i * tile_rows, (i + 1) * tile_rows)
                    rows[-1][:, lanes] = row_matrices[pairs[bases[depth]][0]]
                    spread[-1][bases[depth], lanes] = 1.0
    rows = jnp.asarray(np.stack(rows))
    spread = jnp.asarray(np.concatenate(spread, axis=1), BF16)
    block_rows = PD * tile_rows + EXTRA
    first, second, third = factors
    messages = [
        jax.ShapeDtypeStruct(((high - low) * second, block_rows, tile_side), BF16)
        for _ in range(first) for low, high in send_groups(third)]
    return pl.pallas_call(
        functools.partial(smooth_kernel, factors=factors, row_count=row_count,
            layers=layers),
        in_specs=[SMEM] + [pl.BlockSpec(memory_space=pltpu.HBM)] * 9,
        out_specs=[VMEM] * (1 + len(messages)),
        out_shape=[jax.ShapeDtypeStruct(images.shape, F32)] + messages,
        scratch_shapes=[
            *(pltpu.SMEM(value.shape, value.dtype) for value in (weights, valid_epoch, owners, locals_)),
            *(pltpu.VMEM(value.shape, value.dtype) for value in (coeffs, spread, columns, rows, images)),
            pltpu.SemaphoreType.DMA((8,)),
            pltpu.SemaphoreType.DMA((epochs,)),
            pltpu.VMEM((band_count * PD, tile_rows + 8, tile_side), F32),
            pltpu.VMEM((len(layers), P_SIZE * epochs, tile_side), F32),
        ] + [
            pltpu.VMEM((-(-row_count // per_lanes), 2 * tile_rows, tile_side), BF16),
        ] * (2 * TOGETHER) + [
            pltpu.VMEM((per_epoch, row_count * tile_rows, tile_side), BF16),
        ] * (2 * TOGETHER),
        compiler_params=pltpu.CompilerParams(vmem_limit_bytes=VMEM_SMOOTH),
        name="smooth",
    )(me, *[pltpu.with_memory_space_constraint(value, pltpu.HBM) for value in (
        weights, valid_epoch, owners, locals_, coeffs, spread, columns, rows, images)])


def add_kernel(*refs, count, groups, minor):
    parts, outs = refs[:count], refs[count:]
    per_group = outs[0].shape[0]
    for g in range(groups):
        for i in range(per_group):
            place = i * groups + g if minor else g * per_group + i
            total = parts[0][place].astype(F32)
            for part in parts[1:]:
                total = total + part[place].astype(F32)
            outs[g][i] = total.astype(BF16)


def add_and_split(parts, groups, minor=False):
    blocks, block_rows, lanes = parts[0].shape
    out = jax.ShapeDtypeStruct((blocks // groups, block_rows, lanes), BF16)
    return pl.pallas_call(
        functools.partial(add_kernel, count=len(parts), groups=groups, minor=minor),
        in_specs=[VMEM] * len(parts), out_specs=[VMEM] * groups,
        out_shape=[out] * groups, name="add_and_split",
        compiler_params=pltpu.CompilerParams(vmem_limit_bytes=VMEM_SMALL),
    )(*parts)


def finish_kernel(*refs):
    *parts, out_ref = refs
    tile_rows = out_ref.shape[1]
    total = parts[0][0].astype(F32)
    for part in parts[1:]:
        total = total + part[0].astype(F32)
    marks = total[PD * tile_rows:, :]
    inverse = jnp.broadcast_to(1.0 / (1.0 + jnp.sum(marks, axis=1, keepdims=True)), marks.shape)
    for q in range(PD):
        out_ref[q] = (total[q * tile_rows:(q + 1) * tile_rows] * inverse[q:q + 1]).astype(BF16)


def finish(parts, tile_rows):
    return pl.pallas_call(
        finish_kernel, in_specs=[VMEM] * len(parts), out_specs=VMEM,
        out_shape=jax.ShapeDtypeStruct((PD, tile_rows, parts[0].shape[2]), BF16), name="finish",
        compiler_params=pltpu.CompilerParams(vmem_limit_bytes=VMEM_SMALL),
    )(*parts)


def join_kernel(*refs):
    start = 0
    for piece in refs[:-1]:
        refs[-1][start:start + piece.shape[0]] = piece[...]
        start += piece.shape[0]


def join(pieces):
    total = sum(piece.shape[0] for piece in pieces)
    return pl.pallas_call(
        join_kernel, in_specs=[VMEM] * len(pieces), out_specs=VMEM,
        out_shape=jax.ShapeDtypeStruct((total, *pieces[0].shape[1:]), BF16), name="join",
        compiler_params=pltpu.CompilerParams(vmem_limit_bytes=VMEM_SMALL),
    )(*pieces)


def difference_kernel(me_ref, scale_ref, owner_ref, local_ref, smooth_ref, *rest, factors, count):
    pieces, (out_ref, template_ref, table_ref, ready_ref, sems) = rest[:count], rest[count:]
    epochs, per_epoch = smooth_ref.shape[:2]
    start = 0
    for piece in pieces:
        table_ref[start:start + piece.shape[0]] = piece[...]
        start += piece.shape[0]

    def copy(e):
        return pltpu.make_async_copy(ready_ref.at[e], out_ref.at[e], sems.at[e])

    for e in range(epochs):
        scale = scale_ref[0, e]
        for t in range(per_epoch):
            place = place_of(owner_ref[e, t] ^ me_ref[0], factors) * PD + local_ref[e, t]
            ready_ref[e, t] = smooth_ref[e, t] - scale * table_ref[place].astype(F32)
        if e > 0:
            copy(e - 1).start()
    template_ref[...] = table_ref[:PD]
    copy(epochs - 1).start()
    for e in range(epochs):
        copy(e).wait()


def subtract(me, scales, owners, locals_, pieces, smoothed, factors):
    tile_rows, tile_side = smoothed.shape[2:]
    own = (PD, tile_rows, tile_side)
    return pl.pallas_call(
        functools.partial(difference_kernel, factors=factors, count=len(pieces)),
        in_specs=[SMEM] * 4 + [VMEM] * (1 + len(pieces)),
        out_specs=[pl.BlockSpec(memory_space=pltpu.HBM), VMEM],
        out_shape=[jax.ShapeDtypeStruct(smoothed.shape, F32), jax.ShapeDtypeStruct(own, BF16)],
        scratch_shapes=[
            pltpu.VMEM((PD * int(np.prod(factors)), tile_rows, tile_side), BF16),
            pltpu.VMEM(smoothed.shape, F32),
            pltpu.SemaphoreType.DMA((smoothed.shape[0],)),
        ],
        compiler_params=pltpu.CompilerParams(vmem_limit_bytes=VMEM_SUBTRACT),
        name="subtract",
    )(me, scales, owners, locals_, smoothed, *pieces)


TOGETHER = 4
VMEM_SMOOTH = 48 * 1024 * 1024
VMEM_SMALL = 16 * 1024 * 1024
VMEM_SUBTRACT = 40 * 1024 * 1024


def body(images, coeffs, weights, scales, valid_epoch, patch_owner, patch_local):
    band_count = lax.axis_size("band")
    _, epochs, per_epoch, tile_rows, _ = images.shape
    up = gather_stages(band_count)
    me = lax.axis_index("band").astype(jnp.int32).reshape(1)
    owners = patch_owner.reshape(epochs, per_epoch)
    locals_ = patch_local.reshape(epochs, per_epoch)

    smoothed, *messages = smooth(
        me, coeffs[0].transpose(2, 0, 1), weights, valid_epoch, owners, locals_, images[0], up, band_count)

    def exchange(value, step):
        return lax.ppermute(value, "band", [(d, d ^ step) for d in range(band_count)])

    first, second, third = up
    half = third // 2
    stride = first * second
    groups = send_groups(third)
    arrived = []
    for g, (low, high) in enumerate(groups):
        parts = [messages[g]] + [
            exchange(messages[j * len(groups) + g], j) for j in range(1, first)]
        split = add_and_split(parts, second, minor=True)
        parts = [split[0]] + [exchange(split[j], j * first) for j in range(1, second)]
        split = add_and_split(parts, high - low)
        for digit in reversed(range(low, high)):
            block = split[digit - low]
            arrived.append(exchange(block, digit * stride) if digit else block)

    pieces = [finish(arrived, tile_rows)]
    own = pieces[0]
    distant = [exchange(own, j * stride) for j in reversed(range(half, third))][::-1]
    close = [own] + [exchange(own, j * stride) for j in range(1, half)]
    halves = [join(close) if len(close) > 1 else close[0], join(distant) if len(distant) > 1 else distant[0]]
    pieces = []
    for piece in halves:
        pieces.append([piece] + [exchange(piece, j * first) for j in range(1, second)])
    pieces = [piece for pair in zip(*pieces) for piece in pair]
    pieces = pieces + [exchange(piece, j) for j in range(1, first) for piece in pieces]

    difference, templates = subtract(me, scales, owners, locals_, pieces, smoothed, up)
    return difference[None], templates


def solution(mesh):
    return jax.shard_map(
        body,
        mesh=mesh,
        in_specs=(
            P(("groups", "band"), None, None, None, None),
            P(("groups", "band"), None, None, None),
            P(("groups", "band"), None),
            P(("groups", "band"), None),
            P(("groups", "band"), None),
            P(("groups", "band"), None, None, None),
            P(("groups", "band"), None, None),
        ),
        out_specs=(
            P(("groups", "band"), None, None, None, None),
            P(("groups", "band"), None, None),
        ),
        check_vma=False,
    )
```
